256 devices in a mesh: azim: 32 (over z, y_lo, core), rad: 4 (over x), axial: 2 (over y_hi).
Axes of the slice: x: 4, y: 4 (y_hi: 2, y_lo: 2; y = y_hi * 2 + y_lo), z: 8, core: 2. Of those that a mesh axis runs over, the one named last changes fastest.
Arguments:
- adjoint_final: float32 [4, 48, 64, 8, 512], P(None, None, 'azim', 'axial', 'rad'), may hold values from -6 to 6
- state_start: bfloat16 [4, 48, 64, 8, 512], P(None, None, 'azim', 'axial', 'rad'), may hold values from 0.099609375 to 2
- state_middle: bfloat16 [4, 48, 64, 8, 512], P(None, None, 'azim', 'axial', 'rad'), may hold values from 0.099609375 to 2
- speeds: float32 [3, 64, 8, 512], P(None, 'azim', 'axial', 'rad'), may hold values from 0.04 to 0.25
- flags: int32 [3, 64, 8, 512], P(None, 'azim', 'axial', 'rad'), may hold values from 0 to 1
- zones: int32 [64, 8, 512], P('azim', 'axial', 'rad'), may hold values from 0 to 3
- growth_rate: float32 [48], replicated, may hold values from 0.05 to 0.5
- transfer_rate: float32 [48], replicated, may hold values from 0.05 to 0.5
- nucleation_rate: float32 [4], replicated, may hold values from 0.2 to 1
Outputs:
- adjoint_start: float32 [4, 48, 64, 8, 512], P(None, None, 'azim', 'axial', 'rad')
The draws below stay inside these ranges and needn't reach their ends.
All inputs are finite; a program needn't handle non-finite values.
Results may differ from the reference program's by a relative error of at most 0.0003.
Values sent between devices are 32-bit elements; how exact they have to be, the bound alone decides.
A program may use at most 128 MiB of HBM per device.

```python
import math
import jax
import jax.numpy as jnp
from jax import lax

MOMS = 4
SECTIONS = 48
ZONES = 4
NA = 64
NZ = 8
NR = 512


def place_ends(result, rng, least, top_value):
    dims = result.shape
    spot = [jax.random.randint(jax.random.fold_in(rng, axis), (), 0, dims[axis]) for axis in range(len(dims))]
    result = result.at[tuple(spot)].set(least)
    longest = dims.index(max(dims))
    spot[longest] = (spot[longest] + 1) % dims[longest]
    return result.at[tuple(spot)].set(top_value)


def levels(stream_key, extent, cuts, low, largest):
    factor_of = 1.0
    for position, parts in cuts:
        heights = jax.random.uniform(jax.random.fold_in(jax.random.fold_in(stream_key, 6), position), (parts,), jnp.float32, low / len(cuts), largest / len(cuts))
        factor_of = factor_of * jnp.repeat(jnp.exp(heights), extent[position] // parts).reshape((-1,) + (1,) * (len(extent) - 1 - position))
    return factor_of


def normal_values(key, extent, deviation, most, cuts=(), held_as=jnp.bfloat16):
    values = jax.random.normal(key, extent, jnp.float32) * deviation
    if len(cuts) > 0:
        values = levels(key, extent, cuts, -0.22, 0.18) * values
    return jnp.clip(values, min=-most, max=most).astype(held_as)


def setup_inputs(seed: int = 0) -> dict:
    splits = jax.random.split(jax.random.key(seed), 10)
    return {
        "adjoint_final": normal_values(splits[0], (MOMS, SECTIONS, NA, NZ, NR), 1.0, 6.0, ((2, 32), (3, 2), (4, 4)), jnp.float32),
        "state_start": jnp.clip(jnp.exp(math.log(2.0) - 2.9996462 * jax.random.uniform(splits[1], (MOMS, SECTIONS, NA, NZ, NR), jnp.float32) ** levels(splits[1], (MOMS, SECTIONS, NA, NZ, NR), ((2, 32), (3, 2), (4, 4)), -0.2, 0.2)), 0.099609375, 2.0).astype(jnp.bfloat16),
        "state_middle": jnp.clip(jnp.exp(math.log(2.0) - 2.9996462 * jax.random.uniform(splits[2], (MOMS, SECTIONS, NA, NZ, NR), jnp.float32) ** levels(splits[2], (MOMS, SECTIONS, NA, NZ, NR), ((2, 32), (3, 2), (4, 4)), -0.2, 0.2)), 0.099609375, 2.0).astype(jnp.bfloat16),
        "speeds": jnp.clip(jnp.exp(math.log(0.25) - 1.8325815 * jax.random.uniform(splits[3], (3, NA, NZ, NR), jnp.float32) ** levels(splits[3], (3, NA, NZ, NR), ((1, 32), (2, 2), (3, 4)), -0.2, 0.2)), 0.04, 0.25),
        "flags": place_ends(jax.random.randint(splits[4], (3, NA, NZ, NR), 0, 2), jax.random.fold_in(splits[4], 1), 0, 1).astype(jnp.int32),
        "zones": place_ends(jax.random.randint(splits[5], (NA, NZ, NR), 0, ZONES), jax.random.fold_in(splits[5], 1), 0, ZONES - 1).astype(jnp.int32),
        "growth_rate": jnp.clip(jnp.exp(jax.random.uniform(splits[6], (SECTIONS,), jnp.float32, math.log(0.05), math.log(0.5))), 0.05, 0.5),
        "transfer_rate": jnp.clip(jnp.exp(jax.random.uniform(splits[7], (SECTIONS,), jnp.float32, math.log(0.05), math.log(0.5))), 0.05, 0.5),
        "nucleation_rate": jnp.clip(jnp.exp(jax.random.uniform(splits[8], (ZONES,), jnp.float32, math.log(0.2), math.log(1.0))), 0.2, 1.0),
    }


supersat_scale = 1.5
crowding = 0.02
nucleus_moments = (1.0, 0.5, 0.25, 0.125)

def source_term(state, growth_rate, transfer_rate, nucleation):
    extra = (1,) * (state.ndim - 2)
    growth = growth_rate.reshape((1, -1) + extra)
    transfer = transfer_rate.reshape((1, -1) + extra)
    third = state[3]
    sigma = supersat_scale / (1.0 + crowding * lax.optimization_barrier(jnp.sum(third * third, axis=0)))
    lower = jnp.concatenate([jnp.zeros_like(state[0:1]), state[:3]], axis=0)
    factors = jnp.array([0.0, 1.0, 2.0, 3.0], dtype=state.dtype).reshape((4, 1) + extra)
    outflow = transfer * state
    inflow = jnp.concatenate([jnp.zeros_like(outflow[:, 0:1]), outflow[:, :-1]], axis=1)
    first = (jnp.arange(state.shape[1]) == 0).astype(state.dtype).reshape((1, -1) + extra)
    nucleus = jnp.array(nucleus_moments, dtype=state.dtype).reshape((4, 1) + extra)
    birth = nucleus * first * (nucleation * sigma * sigma)[None, None]
    return sigma[None, None] * (factors * growth * lower + inflow - outflow) + birth

def source_adjoint(state, adjoint, growth_rate, transfer_rate, nucleation):
    _, pull = jax.vjp(lambda field: source_term(field, growth_rate, transfer_rate, nucleation), state)
    return pull(adjoint)[0]

def cut_region(field, direction, offset):
    lead = [slice(None)] * (field.ndim - 3)
    spatial = []
    for which in range(3):
        moved = offset if which == direction else 0
        length = field.shape[field.ndim - 3 + which]
        spatial.append(slice(1 + moved, length - 1 + moved))
    return field[tuple(lead + spatial)]

def transport_adjoint(adjoint_pad, coeff_pad):
    total = None
    for direction in range(3):
        centre = cut_region(adjoint_pad, direction, 0)
        higher = cut_region(adjoint_pad, direction, 1)
        lowerv = cut_region(adjoint_pad, direction, -1)
        p_high = cut_region(coeff_pad[direction], direction, 1)
        q_here = cut_region(coeff_pad[3 + direction], direction, 0)
        term = p_high * (higher - centre) + q_here * (lowerv - centre)
        total = term if total is None else total + term
    return total

def face_coefficients(speeds, flags):
    upwind = flags.astype(speeds.dtype)
    return jnp.concatenate([speeds * upwind, speeds * (1.0 - upwind)], axis=0)

def nucleation_field(zones, nucleation_rate):
    labels = jnp.arange(nucleation_rate.shape[0], dtype=jnp.int32).reshape((-1, 1, 1, 1))
    match = (zones[None] == labels).astype(nucleation_rate.dtype)
    return lax.optimization_barrier(jnp.sum(match * nucleation_rate.reshape((-1, 1, 1, 1)), axis=0))

def pad_field(field):
    count = field.ndim
    wrapped = jnp.pad(field, [(0, 0)] * (count - 3) + [(1, 1), (0, 0), (0, 0)], mode='wrap')
    return jnp.pad(wrapped, [(0, 0)] * (count - 2) + [(1, 1), (1, 1)])

def reference(adjoint_final, state_start, state_middle, speeds, flags, zones, growth_rate, transfer_rate, nucleation_rate):
    coeff_pad = pad_field(face_coefficients(speeds, flags))
    nucleation = nucleation_field(zones, nucleation_rate)
    start = state_start.astype(jnp.float32)
    middle = state_middle.astype(jnp.float32)
    later = adjoint_final
    adjoint_middle = 0.5 * later + 0.5 * (transport_adjoint(pad_field(later), coeff_pad) + source_adjoint(middle, later, growth_rate, transfer_rate, nucleation))
    return 0.5 * later + adjoint_middle + transport_adjoint(pad_field(adjoint_middle), coeff_pad) + source_adjoint(start, adjoint_middle, growth_rate, transfer_rate, nucleation)
```

```python
import functools

import jax
import jax.numpy as jnp
from jax import lax
from jax.experimental import pallas as pl
from jax.experimental.pallas import tpu as pltpu
from jax.sharding import PartitionSpec as P

supersat_scale = 1.5
crowding = 0.02
MESH = pl.DeviceIdType.MESH
F32 = jnp.float32


def rolled(x, shift, axis):
    return pltpu.roll(x, shift, axis)


def shifted(axis, step):
    size = lax.axis_size(axis)
    return {axis: lax.rem(lax.axis_index(axis) + step + size, size)}


def kernel(
    far_ref, af_ref, sm_ref, ss_ref, speeds_ref, flags_ref, zones_ref, growth_ref, transfer_ref, nucl_ref,
    out_ref,
    a_v, b_v, o_v, sm_v, ss_v, sp_v, fl_v, zn_v, g_s, t_s, n_s,
    pz_src, pz_dst,
    az_src, az_one, az_two,
    ax_src1, ax_dst1, ax_src2, ax_dst2,
    rd_src1, rd_dst1, rd_src2, rd_dst2,
    local_sem, send_sem, recv_sem, out_sem,
):
    sections = sm_ref.shape[1]
    above, below = shifted("azim", 1), shifted("azim", -1)
    right, left = shifted("rad", 1), shifted("rad", -1)
    other = shifted("axial", 1)
    first_half = lax.axis_index("axial") == 0

    def remote(n, src, dst, device):
        return pltpu.make_async_remote_copy(
            src_ref=src, dst_ref=dst, send_sem=send_sem.at[n], recv_sem=recv_sem.at[n],
            device_id=device, device_id_type=MESH,
        )

    loads = [
        pltpu.make_async_copy(src, dst, local_sem.at[n])
        for n, (src, dst) in enumerate([
            (speeds_ref, sp_v), (flags_ref, fl_v), (af_ref, a_v.at[:, 0:sections]),
            (zones_ref, zn_v), (growth_ref, g_s), (transfer_ref, t_s), (nucl_ref, n_s),
            (sm_ref, sm_v), (ss_ref, ss_v),
        ])
    ]
    barrier = pltpu.get_barrier_semaphore()
    for device in (above, below, right, left, other):
        pl.semaphore_signal(barrier, inc=1, device_id=device, device_id_type=MESH)
    for copy in loads:
        copy.start()
    pl.semaphore_wait(barrier, 5)

    up1 = remote(0, far_ref.at[:, :, 1], az_one.at[:, :, 0], above)
    down1 = remote(1, far_ref.at[:, :, 0], az_one.at[:, :, 1], below)
    up1.start()
    down1.start()

    row = lax.broadcasted_iota(jnp.int32, (8, 128), 0)
    lane = lax.broadcasted_iota(jnp.int32, (8, 128), 1)
    arow = lax.rem(row, 4)
    edge = jnp.where(first_half, 3, 0)

    def pack_axial(values):
        packed = values[0]
        for k in range(1, 4):
            packed = jnp.where(arow == lax.rem(edge + k, 4), rolled(values[k], k, 0), packed)
        return packed

    def pack_radial(s, values, packs):
        here = lax.shift_right_logical(lane, 1) == s
        return [jnp.where(here, rolled(x, 2 * s + 1, 1), pack) for x, pack in zip(values, packs)]

    zero = jnp.zeros((8, 128), F32)

    loads[0].wait()
    loads[1].wait()
    upwind = fl_v[...].astype(F32)
    speeds = sp_v[...]
    p = speeds * upwind
    q = speeds * (1.0 - upwind)
    pz_src[...] = p[0]
    ax_src1[sections] = p[1]
    rd_src1[4] = p[2]
    pz = remote(2, pz_src, pz_dst, below)
    pz.start()

    loads[2].wait()
    a_v[:, sections] = jnp.zeros((4, 8, 128), F32)
    b_v[:, sections] = jnp.zeros((4, 8, 128), F32)

    def pack_first(s, packs):
        values = [a_v[k, s] for k in range(4)]
        ax_src1[s] = pack_axial(values)
        return pack_radial(s, values, packs)

    packs = lax.fori_loop(0, sections, pack_first, [zero] * 4)
    for k in range(4):
        rd_src1[k] = packs[k]
    ax1 = remote(3, ax_src1, ax_dst1, other)
    rr1 = remote(4, rd_src1, rd_dst1.at[0], right)
    rl1 = remote(5, rd_src1, rd_dst1.at[1], left)
    ax1.start()
    rr1.start()
    rl1.start()

    for copy in loads[3:7]:
        copy.wait()
    zones = zn_v[...]
    nucleation = zero
    for z in range(nucl_ref.shape[0]):
        nucleation = nucleation + jnp.where(zones == z, n_s[z], 0.0)
    loads[7].wait()

    def slope(s, k, values, after):
        t = t_s[s]
        term = t * (after - values[k])
        if k < 3:
            term = term + ((k + 1) * g_s[s]) * values[k + 1]
        return term

    def source_sums(s, values, after, state, sums):
        gain, third = sums
        for k in range(4):
            u = state[k, s].astype(F32)
            gain = gain + u * slope(s, k, values, after[k])
            if k == 3:
                third = third + u * u
        return gain, third

    def source_scalars(sums, first):
        gain, third = sums
        sigma = supersat_scale / (1.0 + crowding * third)
        birth = first[0] + 0.5 * first[1] + 0.25 * first[2] + 0.125 * first[3]
        total = gain + 2.0 * sigma * nucleation * birth
        return sigma, (-2.0 * crowding / supersat_scale) * sigma * sigma * total

    def first_sums(s, sums):
        values = [a_v[k, s] for k in range(4)]
        after = [a_v[k, s + 1] for k in range(4)]
        return source_sums(s, values, after, sm_v, sums)

    sums = lax.fori_loop(0, sections, first_sums, (zero, zero))
    sigma1, third1 = source_scalars(sums, [a_v[k, 0] for k in range(4)])

    ax1.wait_recv()
    rr1.wait_recv()
    rl1.wait_recv()
    p0, p1, p2 = p[0], p[1], p[2]
    q0, q1, q2 = q[0], q[1], q[2]
    c_mid = jnp.where(row < 4, rolled(p0, 4, 0), q0)
    c_up = jnp.where(arow < 3, rolled(p1, 7, 0), 0.0)
    c_low = jnp.where(arow > 0, q1, 0.0)
    far_face = jnp.where(first_half, rolled(ax_dst1[sections], 3, 0), 0.0)
    ax_all = jnp.where(arow == 0, q1, jnp.where(arow == 3, far_face, 0.0))
    ax_halo = jnp.where(arow == edge, ax_all, 0.0)
    c_right = jnp.where(lane < 127, rolled(p2, 127, 1), 0.0)
    c_left = jnp.where(lane > 0, q2, 0.0)
    rad_index = lax.axis_index("rad")
    rad_last = lax.axis_size("rad") - 1
    rd_high = jnp.where(rad_index < rad_last, rolled(rd_dst1[1, 4], 127, 1), 0.0)
    rd_all = jnp.where(lane == 0, q2, jnp.where(lane == 127, rd_high, 0.0))
    rd_halo = jnp.where((lane == 0) & (rad_index == 0), 0.0, rd_all)
    diagonal = c_mid + c_up + c_low + ax_all + c_right + c_left + rd_all

    def radial_halos(dst):
        even = lax.rem(lane, 2) == 0
        return [jnp.where(even, dst[0, k], rolled(dst[1, k], 126, 1)) for k in range(4)]

    def axial_halo(packed):
        return jnp.where(first_half, rolled(packed, 3, 0), rolled(packed, 5, 0))

    def outside(s, k, axial, radial):
        shift = lax.rem(128 - 2 * s, 128)
        there = axial if k == 0 else rolled(axial, 8 - k, 0)
        return there, rolled(radial[k], shift, 1)

    def inside(x, mid, up, low, right_c, left_c):
        return (
            mid * rolled(x, 4, 0)
            + up * rolled(x, 7, 0)
            + low * rolled(x, 1, 0)
            + right_c * rolled(x, 127, 1)
            + left_c * rolled(x, 1, 1)
        )

    radial1 = radial_halos(rd_dst1)
    keep1 = 0.5 * (1.0 - diagonal)
    half = [0.5 * c for c in (c_mid, c_up, c_low, c_right, c_left)]
    half_ax, half_rd = 0.5 * ax_halo, 0.5 * rd_halo
    half_sigma, half_third = 0.5 * sigma1, 0.5 * third1

    def first_stage(s, carry):
        values = [a_v[k, s] for k in range(4)]
        axial = axial_halo(ax_dst1[s])
        for k in range(4):
            x = values[k]
            ax, rd = outside(s, k, axial, radial1)
            y = keep1 * x + inside(x, *half) + half_ax * ax + half_rd * rd
            y = y + half_sigma * slope(s, k, values, a_v[k, s + 1])
            if k == 3:
                y = y + half_third * sm_v[3, s].astype(F32)
            b_v[k, s] = y
            az_src[0, k, s] = y[0:4]
            az_src[1, k, s] = y[4:8]
        return carry

    lax.fori_loop(0, sections, first_stage, 0)
    up2 = remote(6, az_src.at[1], az_two.at[:, :, 0], above)
    down2 = remote(7, az_src.at[0], az_two.at[:, :, 1], below)
    up2.start()
    down2.start()

    pz.wait_recv()
    az_halo = jnp.where(row < 4, q0, rolled(pz_dst[...], 4, 0))
    half_az = 0.5 * az_halo
    up1.wait_recv()
    down1.wait_recv()
    loads[8].wait()

    def halo_planes(ref, k, s):
        return jnp.concatenate([ref[k, s, 0], ref[k, s, 1]], axis=0)

    def middle_stage(i, carry):
        packs, after, sums = carry
        s = sections - 1 - i
        values = []
        for k in range(4):
            y = b_v[k, s] + half_az * (halo_planes(az_one, k, s) - a_v[k, s])
            b_v[k, s] = y
            values.append(y)
        ax_src2[s] = pack_axial(values)
        packs = pack_radial(s, values, packs)
        sums = source_sums(s, values, after, ss_v, sums)
        return packs, values, sums

    packs, head, sums = lax.fori_loop(
        0, sections, middle_stage, ([zero] * 4, [zero] * 4, (zero, zero))
    )
    for k in range(4):
        rd_src2[k] = packs[k]
    ax2 = remote(8, ax_src2, ax_dst2, other)
    rr2 = remote(9, rd_src2, rd_dst2.at[0], right)
    rl2 = remote(10, rd_src2, rd_dst2.at[1], left)
    ax2.start()
    rr2.start()
    rl2.start()
    sigma2, third2 = source_scalars(sums, head)
    keep2 = 1.0 - (diagonal + az_halo)

    def second_stage(s, carry):
        values = [b_v[k, s] for k in range(4)]
        for k in range(4):
            x = values[k]
            y = keep2 * x + 0.5 * a_v[k, s] + inside(x, c_mid, c_up, c_low, c_right, c_left)
            y = y + sigma2 * slope(s, k, values, b_v[k, s + 1])
            if k == 3:
                y = y + third2 * ss_v[3, s].astype(F32)
            o_v[k, s] = y
        return carry

    lax.fori_loop(0, sections, second_stage, 0)
    rr2.wait_recv()
    rl2.wait_recv()
    radial2 = radial_halos(rd_dst2)
    up2.wait_recv()
    down2.wait_recv()
    ax2.wait_recv()

    def last_stage(s, carry):
        axial = axial_halo(ax_dst2[s])
        for k in range(4):
            ax, rd = outside(s, k, axial, radial2)
            o_v[k, s] = o_v[k, s] + az_halo * halo_planes(az_two, k, s) + ax_halo * ax + rd_halo * rd
        return carry

    lax.fori_loop(0, sections, last_stage, 0)
    store = pltpu.make_async_copy(o_v, out_ref, out_sem)
    store.start()
    for copy in (up1, down1, pz, ax1, rr1, rl1, up2, down2, ax2, rr2, rl2):
        copy.wait_send()
    store.wait()


def shards(
    adjoint_final,
    state_start,
    state_middle,
    speeds,
    flags,
    zones,
    growth_rate,
    transfer_rate,
    nucleation_rate,
):
    dims = adjoint_final.shape
    moms, sections = dims[0], dims[1]
    flat = (moms, sections, 8, 128)
    hbm = pl.BlockSpec(memory_space=pltpu.MemorySpace.HBM)
    vmem = pltpu.VMEM
    dma = pltpu.SemaphoreType.DMA
    out = pl.pallas_call(
        kernel,
        out_shape=jax.ShapeDtypeStruct(flat, F32),
        in_specs=[hbm] * 10,
        out_specs=hbm,
        scratch_shapes=[
            vmem((moms, sections + 1, 8, 128), F32),
            vmem((moms, sections + 1, 8, 128), F32),
            vmem(flat, F32),
            vmem(flat, jnp.bfloat16),
            vmem(flat, jnp.bfloat16),
            vmem((3, 8, 128), F32),
            vmem((3, 8, 128), jnp.int32),
            vmem((8, 128), jnp.int32),
            pltpu.SMEM(growth_rate.shape, F32),
            pltpu.SMEM(transfer_rate.shape, F32),
            pltpu.SMEM(nucleation_rate.shape, F32),
            vmem((8, 128), F32),
            vmem((8, 128), F32),
            vmem((2, moms, sections, 4, 128), F32),
            vmem((moms, sections, 2, 4, 128), F32),
            vmem((moms, sections, 2, 4, 128), F32),
            vmem((sections + 1, 8, 128), F32),
            vmem((sections + 1, 8, 128), F32),
            vmem((sections, 8, 128), F32),
            vmem((sections, 8, 128), F32),
            vmem((5, 8, 128), F32),
            vmem((2, 5, 8, 128), F32),
            vmem((4, 8, 128), F32),
            vmem((2, 4, 8, 128), F32),
            dma((9,)),
            dma((11,)),
            dma((11,)),
            dma,
        ],
        compiler_params=pltpu.CompilerParams(
            collective_id=0, has_side_effects=True, vmem_limit_bytes=40 << 20
        ),
    )(
        adjoint_final,
        adjoint_final.reshape(flat),
        state_middle.reshape(flat),
        state_start.reshape(flat),
        speeds.reshape(3, 8, 128),
        flags.reshape(3, 8, 128),
        zones.reshape(8, 128),
        growth_rate,
        transfer_rate,
        nucleation_rate,
    )
    return out.reshape(dims)


def solution(mesh):
    return jax.shard_map(
        shards,
        mesh=mesh,
        in_specs=(
            P(None, None, "azim", "axial", "rad"),
            P(None, None, "azim", "axial", "rad"),
            P(None, None, "azim", "axial", "rad"),
            P(None, "azim", "axial", "rad"),
            P(None, "azim", "axial", "rad"),
            P("azim", "axial", "rad"),
            P(),
            P(),
            P(),
        ),
        out_specs=P(None, None, "azim", "axial", "rad"),
        check_vma=False,
    )
```

```python
import functools

import jax
import jax.numpy as jnp
from jax import lax
from jax.experimental import pallas as pl
from jax.experimental.pallas import tpu as pltpu
from jax.sharding import PartitionSpec as P

supersat_scale = 1.5
crowding = 0.02
MESH = pl.DeviceIdType.MESH
F32 = jnp.float32
UNROLL = 16


def rolled(x, shift, axis):
    return pltpu.roll(x, shift, axis)


def shifted(axis, step):
    size = lax.axis_size(axis)
    return {axis: lax.rem(lax.axis_index(axis) + step + size, size)}


def kernel(
    far_ref, af_ref, sm_ref, ss_ref, speeds_ref, flags_ref, zones_ref, growth_ref, transfer_ref, nucl_ref,
    out_ref,
    a_v, b_v, o_v, sm_v, ss_v, sp_v, fl_v, zn_v, g_s, t_s, n_s,
    pz_src, pz_dst,
    az_src, az_one, az_two,
    ax_src1, ax_dst1, ax_src2, ax_dst2,
    rd_src1, rd_dst1, rd_src2, rd_dst2,
    local_sem, send_sem, recv_sem, out_sem,
):
    sections = sm_ref.shape[1]
    above, below = shifted("azim", 1), shifted("azim", -1)
    right, left = shifted("rad", 1), shifted("rad", -1)
    other = shifted("axial", 1)
    first_half = lax.axis_index("axial") == 0

    def sweep(step, init):
        return lax.fori_loop(0, sections, step, init, unroll=UNROLL)

    def remote(n, src, dst, device):
        return pltpu.make_async_remote_copy(
            src_ref=src, dst_ref=dst, send_sem=send_sem.at[n], recv_sem=recv_sem.at[n],
            device_id=device, device_id_type=MESH,
        )

    loads = [
        pltpu.make_async_copy(src, dst, local_sem.at[n])
        for n, (src, dst) in enumerate([
            (speeds_ref, sp_v), (flags_ref, fl_v), (af_ref, a_v.at[:, 0:sections]),
            (zones_ref, zn_v), (growth_ref, g_s), (transfer_ref, t_s), (nucl_ref, n_s),
            (sm_ref, sm_v), (ss_ref, ss_v),
        ])
    ]
    barrier = pltpu.get_barrier_semaphore()
    for device in (above, below, right, left, other):
        pl.semaphore_signal(barrier, inc=1, device_id=device, device_id_type=MESH)
    for copy in loads:
        copy.start()
    pl.semaphore_wait(barrier, 5)

    up1 = remote(0, far_ref.at[:, :, 1], az_one.at[:, :, 0], above)
    down1 = remote(1, far_ref.at[:, :, 0], az_one.at[:, :, 1], below)
    up1.start()
    down1.start()

    row = lax.broadcasted_iota(jnp.int32, (8, 128), 0)
    lane = lax.broadcasted_iota(jnp.int32, (8, 128), 1)
    arow = lax.rem(row, 4)
    edge = jnp.where(first_half, 3, 0)

    def pack_axial(values):
        packed = values[0]
        for k in range(1, 4):
            packed = jnp.where(arow == lax.rem(edge + k, 4), rolled(values[k], k, 0), packed)
        return packed

    def pack_radial(s, values, packs):
        here = lax.shift_right_logical(lane, 1) == s
        return [jnp.where(here, rolled(x, 2 * s + 1, 1), pack) for x, pack in zip(values, packs)]

    zero = jnp.zeros((8, 128), F32)

    loads[0].wait()
    loads[1].wait()
    upwind = fl_v[...].astype(F32)
    speeds = sp_v[...]
    p = speeds * upwind
    q = speeds * (1.0 - upwind)
    pz_src[...] = p[0]
    ax_src1[sections] = p[1]
    rd_src1[4] = p[2]
    pz = remote(2, pz_src, pz_dst, below)
    pz.start()

    loads[2].wait()
    a_v[:, sections] = jnp.zeros((4, 8, 128), F32)
    b_v[:, sections] = jnp.zeros((4, 8, 128), F32)

    def pack_first(s, packs):
        values = [a_v[k, s] for k in range(4)]
        ax_src1[s] = pack_axial(values)
        return pack_radial(s, values, packs)

    packs = sweep(pack_first, [zero] * 4)
    for k in range(4):
        rd_src1[k] = packs[k]
    ax1 = remote(3, ax_src1, ax_dst1, other)
    rr1 = remote(4, rd_src1, rd_dst1.at[0], right)
    rl1 = remote(5, rd_src1, rd_dst1.at[1], left)
    ax1.start()
    rr1.start()
    rl1.start()

    for copy in loads[3:7]:
        copy.wait()
    zones = zn_v[...]
    nucleation = zero
    for z in range(nucl_ref.shape[0]):
        nucleation = nucleation + jnp.where(zones == z, n_s[z], 0.0)
    loads[7].wait()

    def slope(s, k, values, after):
        t = t_s[s]
        term = t * (after - values[k])
        if k < 3:
            term = term + ((k + 1) * g_s[s]) * values[k + 1]
        return term

    def source_sums(s, values, after, state, sums):
        gain, third = sums
        for k in range(4):
            u = state[k, s].astype(F32)
            gain = gain + u * slope(s, k, values, after[k])
            if k == 3:
                third = third + u * u
        return gain, third

    def source_scalars(sums, first):
        gain, third = sums
        sigma = supersat_scale / (1.0 + crowding * third)
        birth = first[0] + 0.5 * first[1] + 0.25 * first[2] + 0.125 * first[3]
        total = gain + 2.0 * sigma * nucleation * birth
        return sigma, (-2.0 * crowding / supersat_scale) * sigma * sigma * total

    def first_sums(s, sums):
        values = [a_v[k, s] for k in range(4)]
        after = [a_v[k, s + 1] for k in range(4)]
        return source_sums(s, values, after, sm_v, sums)

    sums = sweep(first_sums, (zero, zero))
    sigma1, third1 = source_scalars(sums, [a_v[k, 0] for k in range(4)])

    ax1.wait_recv()
    rr1.wait_recv()
    rl1.wait_recv()
    p0, p1, p2 = p[0], p[1], p[2]
    q0, q1, q2 = q[0], q[1], q[2]
    c_mid = jnp.where(row < 4, rolled(p0, 4, 0), q0)
    c_up = jnp.where(arow < 3, rolled(p1, 7, 0), 0.0)
    c_low = jnp.where(arow > 0, q1, 0.0)
    far_face = jnp.where(first_half, rolled(ax_dst1[sections], 3, 0), 0.0)
    ax_all = jnp.where(arow == 0, q1, jnp.where(arow == 3, far_face, 0.0))
    ax_halo = jnp.where(arow == edge, ax_all, 0.0)
    c_right = jnp.where(lane < 127, rolled(p2, 127, 1), 0.0)
    c_left = jnp.where(lane > 0, q2, 0.0)
    rad_index = lax.axis_index("rad")
    rad_last = lax.axis_size("rad") - 1
    rd_high = jnp.where(rad_index < rad_last, rolled(rd_dst1[1, 4], 127, 1), 0.0)
    rd_all = jnp.where(lane == 0, q2, jnp.where(lane == 127, rd_high, 0.0))
    rd_halo = jnp.where((lane == 0) & (rad_index == 0), 0.0, rd_all)
    diagonal = c_mid + c_up + c_low + ax_all + c_right + c_left + rd_all

    def radial_halos(dst):
        even = lax.rem(lane, 2) == 0
        return [jnp.where(even, dst[0, k], rolled(dst[1, k], 126, 1)) for k in range(4)]

    def axial_halo(packed):
        return jnp.where(first_half, rolled(packed, 3, 0), rolled(packed, 5, 0))

    def outside(s, k, axial, radial):
        shift = lax.rem(128 - 2 * s, 128)
        there = axial if k == 0 else rolled(axial, 8 - k, 0)
        return there, rolled(radial[k], shift, 1)

    def inside(x, mid, up, low, right_c, left_c):
        return (
            mid * rolled(x, 4, 0)
            + up * rolled(x, 7, 0)
            + low * rolled(x, 1, 0)
            + right_c * rolled(x, 127, 1)
            + left_c * rolled(x, 1, 1)
        )

    radial1 = radial_halos(rd_dst1)
    keep1 = 0.5 * (1.0 - diagonal)
    half = [0.5 * c for c in (c_mid, c_up, c_low, c_right, c_left)]
    half_ax, half_rd = 0.5 * ax_halo, 0.5 * rd_halo
    half_sigma, half_third = 0.5 * sigma1, 0.5 * third1

    def first_stage(s, carry):
        values = [a_v[k, s] for k in range(4)]
        axial = axial_halo(ax_dst1[s])
        for k in range(4):
            x = values[k]
            ax, rd = outside(s, k, axial, radial1)
            y = keep1 * x + inside(x, *half) + half_ax * ax + half_rd * rd
            y = y + half_sigma * slope(s, k, values, a_v[k, s + 1])
            if k == 3:
                y = y + half_third * sm_v[3, s].astype(F32)
            b_v[k, s] = y
            az_src[0, k, s] = y[0:4]
            az_src[1, k, s] = y[4:8]
        return carry

    sweep(first_stage, 0)
    up2 = remote(6, az_src.at[1], az_two.at[:, :, 0], above)
    down2 = remote(7, az_src.at[0], az_two.at[:, :, 1], below)
    up2.start()
    down2.start()

    pz.wait_recv()
    az_halo = jnp.where(row < 4, q0, rolled(pz_dst[...], 4, 0))
    half_az = 0.5 * az_halo
    up1.wait_recv()
    down1.wait_recv()
    loads[8].wait()

    def halo_planes(ref, k, s):
        return jnp.concatenate([ref[k, s, 0], ref[k, s, 1]], axis=0)

    def middle_stage(i, carry):
        packs, after, sums = carry
        s = sections - 1 - i
        values = []
        for k in range(4):
            y = b_v[k, s] + half_az * (halo_planes(az_one, k, s) - a_v[k, s])
            b_v[k, s] = y
            values.append(y)
        ax_src2[s] = pack_axial(values)
        packs = pack_radial(s, values, packs)
        sums = source_sums(s, values, after, ss_v, sums)
        return packs, values, sums

    packs, head, sums = sweep(middle_stage, ([zero] * 4, [zero] * 4, (zero, zero)))
    for k in range(4):
        rd_src2[k] = packs[k]
    ax2 = remote(8, ax_src2, ax_dst2, other)
    rr2 = remote(9, rd_src2, rd_dst2.at[0], right)
    rl2 = remote(10, rd_src2, rd_dst2.at[1], left)
    ax2.start()
    rr2.start()
    rl2.start()
    sigma2, third2 = source_scalars(sums, head)
    keep2 = 1.0 - (diagonal + az_halo)

    def second_stage(s, carry):
        values = [b_v[k, s] for k in range(4)]
        for k in range(4):
            x = values[k]
            y = keep2 * x + 0.5 * a_v[k, s] + inside(x, c_mid, c_up, c_low, c_right, c_left)
            y = y + sigma2 * slope(s, k, values, b_v[k, s + 1])
            if k == 3:
                y = y + third2 * ss_v[3, s].astype(F32)
            o_v[k, s] = y
        return carry

    sweep(second_stage, 0)
    rr2.wait_recv()
    rl2.wait_recv()
    radial2 = radial_halos(rd_dst2)
    up2.wait_recv()
    down2.wait_recv()
    ax2.wait_recv()

    def last_stage(s, carry):
        axial = axial_halo(ax_dst2[s])
        for k in range(4):
            ax, rd = outside(s, k, axial, radial2)
            o_v[k, s] = o_v[k, s] + az_halo * halo_planes(az_two, k, s) + ax_halo * ax + rd_halo * rd
        return carry

    sweep(last_stage, 0)
    store = pltpu.make_async_copy(o_v, out_ref, out_sem)
    store.start()
    for copy in (up1, down1, pz, ax1, rr1, rl1, up2, down2, ax2, rr2, rl2):
        copy.wait_send()
    store.wait()


def shards(
    adjoint_final,
    state_start,
    state_middle,
    speeds,
    flags,
    zones,
    growth_rate,
    transfer_rate,
    nucleation_rate,
):
    dims = adjoint_final.shape
    moms, sections = dims[0], dims[1]
    flat = (moms, sections, 8, 128)
    hbm = pl.BlockSpec(memory_space=pltpu.MemorySpace.HBM)
    vmem = pltpu.VMEM
    dma = pltpu.SemaphoreType.DMA
    out = pl.pallas_call(
        kernel,
        out_shape=jax.ShapeDtypeStruct(flat, F32),
        in_specs=[hbm] * 10,
        out_specs=hbm,
        scratch_shapes=[
            vmem((moms, sections + 1, 8, 128), F32),
            vmem((moms, sections + 1, 8, 128), F32),
            vmem(flat, F32),
            vmem(flat, jnp.bfloat16),
            vmem(flat, jnp.bfloat16),
            vmem((3, 8, 128), F32),
            vmem((3, 8, 128), jnp.int32),
            vmem((8, 128), jnp.int32),
            pltpu.SMEM(growth_rate.shape, F32),
            pltpu.SMEM(transfer_rate.shape, F32),
            pltpu.SMEM(nucleation_rate.shape, F32),
            vmem((8, 128), F32),
            vmem((8, 128), F32),
            vmem((2, moms, sections, 4, 128), F32),
            vmem((moms, sections, 2, 4, 128), F32),
            vmem((moms, sections, 2, 4, 128), F32),
            vmem((sections + 1, 8, 128), F32),
            vmem((sections + 1, 8, 128), F32),
            vmem((sections, 8, 128), F32),
            vmem((sections, 8, 128), F32),
            vmem((5, 8, 128), F32),
            vmem((2, 5, 8, 128), F32),
            vmem((4, 8, 128), F32),
            vmem((2, 4, 8, 128), F32),
            dma((9,)),
            dma((11,)),
            dma((11,)),
            dma,
        ],
        compiler_params=pltpu.CompilerParams(
            collective_id=0, has_side_effects=True, vmem_limit_bytes=40 << 20
        ),
    )(*[
        pltpu.with_memory_space_constraint(x, pltpu.MemorySpace.HBM)
        for x in (
            adjoint_final,
            adjoint_final.reshape(flat),
            state_middle.reshape(flat),
            state_start.reshape(flat),
            speeds.reshape(3, 8, 128),
            flags.reshape(3, 8, 128),
            zones.reshape(8, 128),
            growth_rate,
            transfer_rate,
            nucleation_rate,
        )
    ])
    return out.reshape(dims)


def solution(mesh):
    return jax.shard_map(
        shards,
        mesh=mesh,
        in_specs=(
            P(None, None, "azim", "axial", "rad"),
            P(None, None, "azim", "axial", "rad"),
            P(None, None, "azim", "axial", "rad"),
            P(None, "azim", "axial", "rad"),
            P(None, "azim", "axial", "rad"),
            P("azim", "axial", "rad"),
            P(),
            P(),
            P(),
        ),
        out_specs=P(None, None, "azim", "axial", "rad"),
        check_vma=False,
    )
```

```python
import functools

import jax
import jax.numpy as jnp
from jax import lax
from jax.experimental import pallas as pl
from jax.experimental.pallas import tpu as pltpu
from jax.sharding import PartitionSpec as P

supersat_scale = 1.5
crowding = 0.02
MESH = pl.DeviceIdType.MESH
F32 = jnp.float32
CHUNKS = 4
REMOTE = 6 * CHUNKS + 6


def shifted(axis, step):
    size = lax.axis_size(axis)
    return {axis: lax.rem(lax.axis_index(axis) + step + size, size)}


def kernel(
    far_ref, af_ref, sm_ref, ss_ref, speeds_ref, flags_ref, zones_ref, growth_ref, transfer_ref, nucl_ref,
    out_ref,
    a_v, b_v, sm_v, ss_v, sp_v, fl_v, zn_v, g_s, t_s, n_s,
    pz_src, pz_dst, pa_src, pa_dst,
    az_src, az_one, az_two,
    ax_src1, ax_dst1, ax_src2, ax_dst2,
    rd_src1, rd_dst1, rd_src2, rd_dst2,
    local_sem, send_sem, recv_sem,
):
    sections = sm_ref.shape[1]
    above, below = shifted("azim", 1), shifted("azim", -1)
    right, left = shifted("rad", 1), shifted("rad", -1)
    other = shifted("axial", 1)
    first_half = lax.axis_index("axial") == 0

    size = sections // CHUNKS
    chunks = [pl.ds(c * size, size) for c in reversed(range(CHUNKS))]

    def sweep(step, init, chunk=None):
        if chunk is None:
            for chunk in chunks:
                init = sweep(step, init, chunk)
            return init
        top = chunk.start + chunk.size - 1
        return lax.fori_loop(0, chunk.size, lambda i, c: step(top - i, c), init, unroll=chunk.size)

    sent = []

    def remote(src, dst, device):
        n = len(sent)
        copy = pltpu.make_async_remote_copy(
            src_ref=src, dst_ref=dst, send_sem=send_sem.at[n], recv_sem=recv_sem.at[n],
            device_id=device, device_id_type=MESH,
        )
        copy.start()
        sent.append(copy)
        return copy

    loads = [
        pltpu.make_async_copy(src, dst, local_sem.at[n])
        for n, (src, dst) in enumerate([
            (speeds_ref, sp_v), (flags_ref, fl_v), (af_ref, a_v.at[:, 0:sections]),
            (zones_ref, zn_v), (growth_ref, g_s), (transfer_ref, t_s), (nucl_ref, n_s),
            (sm_ref, sm_v), (ss_ref, ss_v),
        ])
    ]
    barrier = pltpu.get_barrier_semaphore()
    for device in (above, below, right, left, other):
        pl.semaphore_signal(barrier, inc=1, device_id=device, device_id_type=MESH)
    for copy in loads:
        copy.start()
    pl.semaphore_wait(barrier, 5)

    planes1 = [
        (
            remote(far_ref.at[:, c, 1], az_one.at[:, c, 0], above),
            remote(far_ref.at[:, c, 0], az_one.at[:, c, 1], below),
        )
        for c in chunks
    ]

    row = lax.broadcasted_iota(jnp.int32, (8, 128), 0)
    lane = lax.broadcasted_iota(jnp.int32, (8, 128), 1)
    arow = lax.rem(row, 4)
    edge = jnp.where(first_half, 3, 0)

    def pack_axial(values):
        packed = values[0]
        for k in range(1, 4):
            packed = jnp.where(arow == lax.rem(edge + k, 4), pltpu.roll(values[k], k, 0), packed)
        return packed

    def pack_radial(s, values, packs):
        here = lax.shift_right_logical(lane, 1) == s
        return [jnp.where(here, pltpu.roll(x, 2 * s + 1, 1), pack) for x, pack in zip(values, packs)]

    zero = jnp.zeros((8, 128), F32)

    loads[0].wait()
    loads[1].wait()
    upwind = fl_v[...].astype(F32)
    speeds = sp_v[...]
    p = speeds * upwind
    q = speeds * (1.0 - upwind)
    pz_src[...] = p[0]
    pa_src[...] = p[1]
    rd_src1[4] = p[2]
    pz = remote(pz_src, pz_dst, below)
    pa = remote(pa_src, pa_dst, other)

    loads[2].wait()
    a_v[:, sections] = jnp.zeros((4, 8, 128), F32)
    b_v[:, sections] = jnp.zeros((4, 8, 128), F32)

    def pack_first(s, packs):
        values = [a_v[k, s] for k in range(4)]
        ax_src1[s] = pack_axial(values)
        return pack_radial(s, values, packs)

    packs, rows1 = [zero] * 4, []
    for c in chunks:
        packs = sweep(pack_first, packs, c)
        rows1.append(remote(ax_src1.at[c], ax_dst1.at[c], other))
    for k in range(4):
        rd_src1[k] = packs[k]
    lanes1 = (
        remote(rd_src1, rd_dst1.at[0], right),
        remote(rd_src1, rd_dst1.at[1], left),
    )

    for copy in loads[3:7]:
        copy.wait()
    zones = zn_v[...]
    nucleation = zero
    for z in range(nucl_ref.shape[0]):
        nucleation = nucleation + jnp.where(zones == z, n_s[z], 0.0)
    loads[7].wait()

    def slope(s, k, values, after):
        t = t_s[s]
        term = t * (after - values[k])
        if k < 3:
            term = term + ((k + 1) * g_s[s]) * values[k + 1]
        return term

    def source_sums(s, values, after, state, sums):
        gain, third = sums
        for k in range(4):
            u = state[k, s].astype(F32)
            gain = gain + u * slope(s, k, values, after[k])
            if k == 3:
                third = third + u * u
        return gain, third

    def source_scalars(sums, first):
        gain, third = sums
        sigma = supersat_scale / (1.0 + crowding * third)
        birth = first[0] + 0.5 * first[1] + 0.25 * first[2] + 0.125 * first[3]
        total = gain + 2.0 * sigma * nucleation * birth
        return sigma, (-2.0 * crowding / supersat_scale) * sigma * sigma * total

    def first_sums(s, sums):
        values = [a_v[k, s] for k in range(4)]
        after = [a_v[k, s + 1] for k in range(4)]
        return source_sums(s, values, after, sm_v, sums)

    sums = sweep(first_sums, (zero, zero))
    sigma1, third1 = source_scalars(sums, [a_v[k, 0] for k in range(4)])

    pa.wait_recv()
    for copy in lanes1:
        copy.wait_recv()
    p0, p1, p2 = p[0], p[1], p[2]
    q0, q1, q2 = q[0], q[1], q[2]
    c_mid = jnp.where(row < 4, pltpu.roll(p0, 4, 0), q0)
    c_up = jnp.where(arow < 3, pltpu.roll(p1, 7, 0), 0.0)
    c_low = jnp.where(arow > 0, q1, 0.0)
    far_face = jnp.where(first_half, pltpu.roll(pa_dst[...], 3, 0), 0.0)
    ax_all = jnp.where(arow == 0, q1, jnp.where(arow == 3, far_face, 0.0))
    ax_halo = jnp.where(arow == edge, ax_all, 0.0)
    c_right = jnp.where(lane < 127, pltpu.roll(p2, 127, 1), 0.0)
    c_left = jnp.where(lane > 0, q2, 0.0)
    rad_index = lax.axis_index("rad")
    rad_last = lax.axis_size("rad") - 1
    rd_high = jnp.where(rad_index < rad_last, pltpu.roll(rd_dst1[1, 4], 127, 1), 0.0)
    rd_all = jnp.where(lane == 0, q2, jnp.where(lane == 127, rd_high, 0.0))
    rd_halo = jnp.where((lane == 0) & (rad_index == 0), 0.0, rd_all)
    diagonal = c_mid + c_up + c_low + ax_all + c_right + c_left + rd_all

    def radial_halos(dst):
        even = lax.rem(lane, 2) == 0
        return [jnp.where(even, dst[0, k], pltpu.roll(dst[1, k], 126, 1)) for k in range(4)]

    def axial_halo(packed):
        return jnp.where(first_half, pltpu.roll(packed, 3, 0), pltpu.roll(packed, 5, 0))

    def outside(s, k, axial, radial):
        shift = lax.rem(128 - 2 * s, 128)
        there = axial if k == 0 else pltpu.roll(axial, 8 - k, 0)
        return there, pltpu.roll(radial[k], shift, 1)

    def inside(x, mid, up, low, right_c, left_c):
        return (
            mid * pltpu.roll(x, 4, 0)
            + up * pltpu.roll(x, 7, 0)
            + low * pltpu.roll(x, 1, 0)
            + right_c * pltpu.roll(x, 127, 1)
            + left_c * pltpu.roll(x, 1, 1)
        )

    radial1 = radial_halos(rd_dst1)
    keep1 = 0.5 * (1.0 - diagonal)
    half = [0.5 * c for c in (c_mid, c_up, c_low, c_right, c_left)]
    half_ax, half_rd = 0.5 * ax_halo, 0.5 * rd_halo
    half_sigma, half_third = 0.5 * sigma1, 0.5 * third1

    def first_stage(s, carry):
        values = [a_v[k, s] for k in range(4)]
        axial = axial_halo(ax_dst1[s])
        for k in range(4):
            x = values[k]
            ax, rd = outside(s, k, axial, radial1)
            y = keep1 * x + inside(x, *half) + half_ax * ax + half_rd * rd
            y = y + half_sigma * slope(s, k, values, a_v[k, s + 1])
            if k == 3:
                y = y + half_third * sm_v[3, s].astype(F32)
            b_v[k, s] = y
            az_src[0, k, s] = y[0:4]
            az_src[1, k, s] = y[4:8]
        return carry

    planes2 = []
    for c, rows in zip(chunks, rows1):
        rows.wait_recv()
        sweep(first_stage, 0, c)
        planes2.append((
            remote(az_src.at[1, :, c], az_two.at[:, c, 0], above),
            remote(az_src.at[0, :, c], az_two.at[:, c, 1], below),
        ))

    pz.wait_recv()
    az_halo = jnp.where(row < 4, q0, pltpu.roll(pz_dst[...], 4, 0))
    half_az = 0.5 * az_halo
    loads[8].wait()

    def halo_planes(ref, k, s):
        return jnp.concatenate([ref[k, s, 0], ref[k, s, 1]], axis=0)

    def middle_stage(s, carry):
        packs, after, sums = carry
        values = []
        for k in range(4):
            y = b_v[k, s] + half_az * (halo_planes(az_one, k, s) - a_v[k, s])
            b_v[k, s] = y
            values.append(y)
        ax_src2[s] = pack_axial(values)
        packs = pack_radial(s, values, packs)
        sums = source_sums(s, values, after, ss_v, sums)
        return packs, values, sums

    carry, rows2 = ([zero] * 4, [zero] * 4, (zero, zero)), []
    for c, planes in zip(chunks, planes1):
        for copy in planes:
            copy.wait_recv()
        carry = sweep(middle_stage, carry, c)
        rows2.append(remote(ax_src2.at[c], ax_dst2.at[c], other))
    packs, head, sums = carry
    for k in range(4):
        rd_src2[k] = packs[k]
    lanes2 = (
        remote(rd_src2, rd_dst2.at[0], right),
        remote(rd_src2, rd_dst2.at[1], left),
    )
    sigma2, third2 = source_scalars(sums, head)
    keep2 = 1.0 - (diagonal + az_halo)

    def second_stage(s, carry):
        values = [b_v[k, s] for k in range(4)]
        for k in range(4):
            x = values[k]
            y = keep2 * x + 0.5 * a_v[k, s] + inside(x, c_mid, c_up, c_low, c_right, c_left)
            y = y + sigma2 * slope(s, k, values, b_v[k, s + 1])
            if k == 3:
                y = y + third2 * ss_v[3, s].astype(F32)
            out_ref[k, s] = y
        return carry

    sweep(second_stage, 0)
    for copy in lanes2:
        copy.wait_recv()
    radial2 = radial_halos(rd_dst2)

    def last_stage(s, carry):
        axial = axial_halo(ax_dst2[s])
        for k in range(4):
            ax, rd = outside(s, k, axial, radial2)
            out_ref[k, s] = out_ref[k, s] + az_halo * halo_planes(az_two, k, s) + ax_halo * ax + rd_halo * rd
        return carry

    for c, planes, rows in zip(chunks, planes2, rows2):
        for copy in (*planes, rows):
            copy.wait_recv()
        sweep(last_stage, 0, c)
    for copy in sent:
        copy.wait_send()


def shards(
    adjoint_final,
    state_start,
    state_middle,
    speeds,
    flags,
    zones,
    growth_rate,
    transfer_rate,
    nucleation_rate,
):
    dims = adjoint_final.shape
    moms, sections = dims[0], dims[1]
    flat = (moms, sections, 8, 128)
    hbm = pl.BlockSpec(memory_space=pltpu.MemorySpace.HBM)
    vmem = pltpu.VMEM
    dma = pltpu.SemaphoreType.DMA
    out = pl.pallas_call(
        kernel,
        out_shape=jax.ShapeDtypeStruct(flat, F32),
        in_specs=[hbm] * 10,
        out_specs=pl.BlockSpec(memory_space=pltpu.VMEM),
        scratch_shapes=[
            vmem((moms, sections + 1, 8, 128), F32),
            vmem((moms, sections + 1, 8, 128), F32),
            vmem(flat, jnp.bfloat16),
            vmem(flat, jnp.bfloat16),
            vmem((3, 8, 128), F32),
            vmem((3, 8, 128), jnp.int32),
            vmem((8, 128), jnp.int32),
            pltpu.SMEM(growth_rate.shape, F32),
            pltpu.SMEM(transfer_rate.shape, F32),
            pltpu.SMEM(nucleation_rate.shape, F32),
            vmem((8, 128), F32),
            vmem((8, 128), F32),
            vmem((8, 128), F32),
            vmem((8, 128), F32),
            vmem((2, moms, sections, 4, 128), F32),
            vmem((moms, sections, 2, 4, 128), F32),
            vmem((moms, sections, 2, 4, 128), F32),
            vmem((sections, 8, 128), F32),
            vmem((sections, 8, 128), F32),
            vmem((sections, 8, 128), F32),
            vmem((sections, 8, 128), F32),
            vmem((5, 8, 128), F32),
            vmem((2, 5, 8, 128), F32),
            vmem((4, 8, 128), F32),
            vmem((2, 4, 8, 128), F32),
            dma((9,)),
            dma((REMOTE,)),
            dma((REMOTE,)),
        ],
        compiler_params=pltpu.CompilerParams(
            collective_id=0, has_side_effects=True, vmem_limit_bytes=40 << 20
        ),
    )(*[
        pltpu.with_memory_space_constraint(x, pltpu.MemorySpace.HBM)
        for x in (
            adjoint_final,
            adjoint_final.reshape(flat),
            state_middle.reshape(flat),
            state_start.reshape(flat),
            speeds.reshape(3, 8, 128),
            flags.reshape(3, 8, 128),
            zones.reshape(8, 128),
            growth_rate,
            transfer_rate,
            nucleation_rate,
        )
    ])
    return out.reshape(dims)


def solution(mesh):
    return jax.shard_map(
        shards,
        mesh=mesh,
        in_specs=(
            P(None, None, "azim", "axial", "rad"),
            P(None, None, "azim", "axial", "rad"),
            P(None, None, "azim", "axial", "rad"),
            P(None, "azim", "axial", "rad"),
            P(None, "azim", "axial", "rad"),
            P("azim", "axial", "rad"),
            P(),
            P(),
            P(),
        ),
        out_specs=P(None, None, "azim", "axial", "rad"),
        check_vma=False,
    )
```

```python
import functools

import jax
import jax.numpy as jnp
from jax import lax
from jax.experimental import pallas as pl
from jax.experimental.pallas import tpu as pltpu
from jax.sharding import PartitionSpec as P

supersat_scale = 1.5
crowding = 0.02
MESH = pl.DeviceIdType.MESH
F32 = jnp.float32
CHUNKS = 4
HOLD = 2
EARLY = 3
EARLY_TWO = 2
HOLD2 = 4
REMOTE = 6 * CHUNKS + 6


def shifted(axis, step):
    size = lax.axis_size(axis)
    return {axis: lax.rem(lax.axis_index(axis) + step + size, size)}


def kernel(
    far_ref, af_ref, sm_ref, ss_ref, speeds_ref, flags_ref, zones_ref, growth_ref, transfer_ref, nucl_ref,
    out_ref,
    a_v, b_v, sm_v, ss_v, sp_v, fl_v, zn_v, g_s, t_s, n_s,
    pz_src, pz_dst, pa_src, pa_dst,
    az_src, az_one, az_two,
    ax_src1, ax_dst1, ax_src2, ax_dst2,
    rd_src1, rd_dst1, rd_src2, rd_dst2,
    local_sem, send_sem, recv_sem,
):
    sections = sm_ref.shape[1]
    above, below = shifted("azim", 1), shifted("azim", -1)
    right, left = shifted("rad", 1), shifted("rad", -1)
    other = shifted("axial", 1)
    first_half = lax.axis_index("axial") == 0

    size = sections // CHUNKS
    chunks = [pl.ds(c * size, size) for c in reversed(range(CHUNKS))]

    def sweep(step, init, chunk=None):
        if chunk is None:
            for chunk in chunks:
                init = sweep(step, init, chunk)
            return init
        top = chunk.start + chunk.size - 1
        return lax.fori_loop(0, chunk.size, lambda i, c: step(top - i, c), init, unroll=chunk.size)

    sent, held = [], []
    place = lax.rem(lax.axis_index("azim"), 4)

    def remote(src, dst, device, hold=None):
        n = len(sent)
        copy = pltpu.make_async_remote_copy(
            src_ref=src, dst_ref=dst, send_sem=send_sem.at[n], recv_sem=recv_sem.at[n],
            device_id=device, device_id_type=MESH,
        )
        if hold is None:
            copy.start()
        else:
            pl.when(jnp.logical_not(hold))(copy.start)
            held.append((hold, copy))
        sent.append(copy)
        return copy

    loads = [
        pltpu.make_async_copy(src, dst, local_sem.at[n])
        for n, (src, dst) in enumerate([
            (speeds_ref, sp_v), (flags_ref, fl_v), (af_ref, a_v.at[:, 0:sections]),
            (zones_ref, zn_v), (growth_ref, g_s), (transfer_ref, t_s), (nucl_ref, n_s),
            (sm_ref, sm_v), (ss_ref, ss_v),
        ])
    ]
    barrier = pltpu.get_barrier_semaphore()
    for device in (above, below, right, left, other):
        pl.semaphore_signal(barrier, inc=1, device_id=device, device_id_type=MESH)
    for copy in loads:
        copy.start()
    pl.semaphore_wait(barrier, 5)

    planes1 = [
        (
            remote(far_ref.at[:, c, 1], az_one.at[:, c, 0], above, place == 1),
            remote(far_ref.at[:, c, 0], az_one.at[:, c, 1], below, place == 2),
        )
        for c in chunks
    ]

    row = lax.broadcasted_iota(jnp.int32, (8, 128), 0)
    lane = lax.broadcasted_iota(jnp.int32, (8, 128), 1)
    arow = lax.rem(row, 4)
    edge = jnp.where(first_half, 3, 0)

    def pack_axial(values):
        packed = values[0]
        for k in range(1, 4):
            packed = jnp.where(arow == lax.rem(edge + k, 4), pltpu.roll(values[k], k, 0), packed)
        return packed

    def pack_radial(s, values, packs):
        here = lax.shift_right_logical(lane, 1) == s
        return [jnp.where(here, pltpu.roll(x, 2 * s + 1, 1), pack) for x, pack in zip(values, packs)]

    zero = jnp.zeros((8, 128), F32)

    loads[0].wait()
    loads[1].wait()
    upwind = fl_v[...].astype(F32)
    speeds = sp_v[...]
    p = speeds * upwind
    q = speeds * (1.0 - upwind)
    pz_src[...] = p[0]
    pa_src[...] = p[1]
    rd_src1[4] = p[2]
    pz = remote(pz_src, pz_dst, below)
    pa = remote(pa_src, pa_dst, other)

    loads[2].wait()
    a_v[:, sections] = jnp.zeros((4, 8, 128), F32)
    b_v[:, sections] = jnp.zeros((4, 8, 128), F32)

    def pack_first(s, packs):
        values = [a_v[k, s] for k in range(4)]
        ax_src1[s] = pack_axial(values)
        return pack_radial(s, values, packs)

    packs, rows1 = [zero] * 4, []
    for c in chunks:
        packs = sweep(pack_first, packs, c)
        rows1.append(remote(ax_src1.at[c], ax_dst1.at[c], other))
    for k in range(4):
        rd_src1[k] = packs[k]
    lanes1 = (
        remote(rd_src1, rd_dst1.at[0], right),
        remote(rd_src1, rd_dst1.at[1], left),
    )

    waits = rows1[:HOLD]
    late = (place == 1) | (place == 2)

    @pl.when(late)
    def _():
        for copy in waits:
            copy.wait_send()

    for hold, copy in held:
        pl.when(hold)(copy.start)

    for copy in loads[3:7]:
        copy.wait()
    zones = zn_v[...]
    nucleation = zero
    for z in range(nucl_ref.shape[0]):
        nucleation = nucleation + jnp.where(zones == z, n_s[z], 0.0)
    loads[7].wait()

    def slope(s, k, values, after):
        t = t_s[s]
        term = t * (after - values[k])
        if k < 3:
            term = term + ((k + 1) * g_s[s]) * values[k + 1]
        return term

    def source_sums(s, values, after, state, sums):
        gain, third = sums
        for k in range(4):
            u = state[k, s].astype(F32)
            gain = gain + u * slope(s, k, values, after[k])
            if k == 3:
                third = third + u * u
        return gain, third

    def source_scalars(sums, first):
        gain, third = sums
        sigma = supersat_scale / (1.0 + crowding * third)
        birth = first[0] + 0.5 * first[1] + 0.25 * first[2] + 0.125 * first[3]
        total = gain + 2.0 * sigma * nucleation * birth
        return sigma, (-2.0 * crowding / supersat_scale) * sigma * sigma * total

    def first_sums(s, sums):
        values = [a_v[k, s] for k in range(4)]
        after = [a_v[k, s + 1] for k in range(4)]
        return source_sums(s, values, after, sm_v, sums)

    sums = sweep(first_sums, (zero, zero))
    sigma1, third1 = source_scalars(sums, [a_v[k, 0] for k in range(4)])

    pa.wait_recv()
    for copy in lanes1:
        copy.wait_recv()
    p0, p1, p2 = p[0], p[1], p[2]
    q0, q1, q2 = q[0], q[1], q[2]
    c_mid = jnp.where(row < 4, pltpu.roll(p0, 4, 0), q0)
    c_up = jnp.where(arow < 3, pltpu.roll(p1, 7, 0), 0.0)
    c_low = jnp.where(arow > 0, q1, 0.0)
    far_face = jnp.where(first_half, pltpu.roll(pa_dst[...], 3, 0), 0.0)
    ax_all = jnp.where(arow == 0, q1, jnp.where(arow == 3, far_face, 0.0))
    ax_halo = jnp.where(arow == edge, ax_all, 0.0)
    c_right = jnp.where(lane < 127, pltpu.roll(p2, 127, 1), 0.0)
    c_left = jnp.where(lane > 0, q2, 0.0)
    rad_index = lax.axis_index("rad")
    rad_last = lax.axis_size("rad") - 1
    rd_high = jnp.where(rad_index < rad_last, pltpu.roll(rd_dst1[1, 4], 127, 1), 0.0)
    rd_all = jnp.where(lane == 0, q2, jnp.where(lane == 127, rd_high, 0.0))
    rd_halo = jnp.where((lane == 0) & (rad_index == 0), 0.0, rd_all)
    diagonal = c_mid + c_up + c_low + ax_all + c_right + c_left + rd_all

    def radial_halos(dst):
        even = lax.rem(lane, 2) == 0
        return [jnp.where(even, dst[0, k], pltpu.roll(dst[1, k], 126, 1)) for k in range(4)]

    def axial_halo(packed):
        return jnp.where(first_half, pltpu.roll(packed, 3, 0), pltpu.roll(packed, 5, 0))

    def row_halo(k, axial):
        return axial if k == 0 else pltpu.roll(axial, 8 - k, 0)

    def radial_halo(s, k, radial):
        return pltpu.roll(radial[k], lax.rem(128 - 2 * s, 128), 1)

    def inside(x, mid, up, low, right_c, left_c):
        return (
            mid * pltpu.roll(x, 4, 0)
            + up * pltpu.roll(x, 7, 0)
            + low * pltpu.roll(x, 1, 0)
            + right_c * pltpu.roll(x, 127, 1)
            + left_c * pltpu.roll(x, 1, 1)
        )

    radial1 = radial_halos(rd_dst1)
    keep1 = 0.5 * (1.0 - diagonal)
    half = [0.5 * c for c in (c_mid, c_up, c_low, c_right, c_left)]
    half_ax, half_rd = 0.5 * ax_halo, 0.5 * rd_halo
    half_sigma, half_third = 0.5 * sigma1, 0.5 * third1

    def first_stage(s, carry):
        values = [a_v[k, s] for k in range(4)]
        axial = axial_halo(ax_dst1[s])
        for k in range(4):
            x = values[k]
            ax, rd = row_halo(k, axial), radial_halo(s, k, radial1)
            y = keep1 * x + inside(x, *half) + half_ax * ax + half_rd * rd
            y = y + half_sigma * slope(s, k, values, a_v[k, s + 1])
            if k == 3:
                y = y + half_third * sm_v[3, s].astype(F32)
            b_v[k, s] = y
            az_src[0, k, s] = y[0:4]
            az_src[1, k, s] = y[4:8]
        return carry

    planes2 = []
    held.clear()

    def later(chunk, one_link, two_links):
        n = [chunk is c for c in chunks].index(True)
        hold = [place == p for p, early in ((one_link, EARLY), (two_links, EARLY_TWO)) if n >= early]
        return functools.reduce(jnp.logical_or, hold) if hold else None

    for c, rows in zip(chunks, rows1):
        rows.wait_recv()
        sweep(first_stage, 0, c)
        planes2.append((
            remote(az_src.at[1, :, c], az_two.at[:, c, 0], above, later(c, 1, 3)),
            remote(az_src.at[0, :, c], az_two.at[:, c, 1], below, later(c, 2, 0)),
        ))

    pz.wait_recv()
    az_halo = jnp.where(row < 4, q0, pltpu.roll(pz_dst[...], 4, 0))
    half_az = 0.5 * az_halo
    loads[8].wait()

    def halo_planes(ref, k, s):
        return jnp.concatenate([ref[k, s, 0], ref[k, s, 1]], axis=0)

    def middle_stage(s, carry):
        packs, after, sums = carry
        values = []
        for k in range(4):
            y = b_v[k, s] + half_az * (halo_planes(az_one, k, s) - a_v[k, s])
            b_v[k, s] = y
            values.append(y)
        ax_src2[s] = pack_axial(values)
        packs = pack_radial(s, values, packs)
        sums = source_sums(s, values, after, ss_v, sums)
        return packs, values, sums

    carry, rows2 = ([zero] * 4, [zero] * 4, (zero, zero)), []
    for c, planes in zip(chunks, planes1):
        for copy in planes:
            copy.wait_recv()
        carry = sweep(middle_stage, carry, c)
        rows2.append(remote(ax_src2.at[c], ax_dst2.at[c], other))
    packs, head, sums = carry
    for k in range(4):
        rd_src2[k] = packs[k]
    lanes2 = (
        remote(rd_src2, rd_dst2.at[0], right),
        remote(rd_src2, rd_dst2.at[1], left),
    )
    sigma2, third2 = source_scalars(sums, head)
    keep2 = 1.0 - (diagonal + az_halo)

    def second_stage(s, carry):
        values = [b_v[k, s] for k in range(4)]
        for k in range(4):
            x = values[k]
            y = keep2 * x + 0.5 * a_v[k, s] + inside(x, c_mid, c_up, c_low, c_right, c_left)
            y = y + sigma2 * slope(s, k, values, b_v[k, s + 1])
            if k == 3:
                y = y + third2 * ss_v[3, s].astype(F32)
            out_ref[k, s] = y
        return carry

    sweep(second_stage, 0)
    for copy in lanes2:
        copy.wait_recv()
    radial2 = radial_halos(rd_dst2)

    def add_lanes(s, carry):
        for k in range(4):
            out_ref[k, s] = out_ref[k, s] + rd_halo * radial_halo(s, k, radial2)
        return carry

    def add_planes(s, carry):
        for k in range(4):
            out_ref[k, s] = out_ref[k, s] + az_halo * halo_planes(az_two, k, s)
        return carry

    def add_rows(s, carry):
        axial = axial_halo(ax_dst2[s])
        for k in range(4):
            out_ref[k, s] = out_ref[k, s] + ax_halo * row_halo(k, axial)
        return carry

    sweep(add_lanes, 0)

    for copy in rows2[:HOLD2]:
        copy.wait_send()
    for hold, copy in held:
        pl.when(hold)(copy.start)

    for c, planes, rows in zip(chunks, planes2, rows2):
        for copy in planes:
            copy.wait_recv()
        sweep(add_planes, 0, c)
        rows.wait_recv()
        sweep(add_rows, 0, c)
    for copy in sent:
        if any(copy is w for w in rows2[:HOLD2]):
            continue
        if any(copy is w for w in waits):
            pl.when(jnp.logical_not(late))(copy.wait_send)
        else:
            copy.wait_send()


def shards(
    adjoint_final,
    state_start,
    state_middle,
    speeds,
    flags,
    zones,
    growth_rate,
    transfer_rate,
    nucleation_rate,
):
    dims = adjoint_final.shape
    moms, sections = dims[0], dims[1]
    flat = (moms, sections, 8, 128)
    hbm = pl.BlockSpec(memory_space=pltpu.MemorySpace.HBM)
    vmem = pltpu.VMEM
    dma = pltpu.SemaphoreType.DMA
    out = pl.pallas_call(
        kernel,
        out_shape=jax.ShapeDtypeStruct(flat, F32),
        in_specs=[hbm] * 10,
        out_specs=pl.BlockSpec(memory_space=pltpu.VMEM),
        scratch_shapes=[
            vmem((moms, sections + 1, 8, 128), F32),
            vmem((moms, sections + 1, 8, 128), F32),
            vmem(flat, jnp.bfloat16),
            vmem(flat, jnp.bfloat16),
            vmem((3, 8, 128), F32),
            vmem((3, 8, 128), jnp.int32),
            vmem((8, 128), jnp.int32),
            pltpu.SMEM(growth_rate.shape, F32),
            pltpu.SMEM(transfer_rate.shape, F32),
            pltpu.SMEM(nucleation_rate.shape, F32),
            vmem((8, 128), F32),
            vmem((8, 128), F32),
            vmem((8, 128), F32),
            vmem((8, 128), F32),
            vmem((2, moms, sections, 4, 128), F32),
            vmem((moms, sections, 2, 4, 128), F32),
            vmem((moms, sections, 2, 4, 128), F32),
            vmem((sections, 8, 128), F32),
            vmem((sections, 8, 128), F32),
            vmem((sections, 8, 128), F32),
            vmem((sections, 8, 128), F32),
            vmem((5, 8, 128), F32),
            vmem((2, 5, 8, 128), F32),
            vmem((4, 8, 128), F32),
            vmem((2, 4, 8, 128), F32),
            dma((9,)),
            dma((REMOTE,)),
            dma((REMOTE,)),
        ],
        compiler_params=pltpu.CompilerParams(
            collective_id=0, has_side_effects=True, vmem_limit_bytes=40 << 20
        ),
    )(*[
        pltpu.with_memory_space_constraint(x, pltpu.MemorySpace.HBM)
        for x in (
            adjoint_final,
            adjoint_final.reshape(flat),
            state_middle.reshape(flat),
            state_start.reshape(flat),
            speeds.reshape(3, 8, 128),
            flags.reshape(3, 8, 128),
            zones.reshape(8, 128),
            growth_rate,
            transfer_rate,
            nucleation_rate,
        )
    ])
    return out.reshape(dims)


def solution(mesh):
    return jax.shard_map(
        shards,
        mesh=mesh,
        in_specs=(
            P(None, None, "azim", "axial", "rad"),
            P(None, None, "azim", "axial", "rad"),
            P(None, None, "azim", "axial", "rad"),
            P(None, "azim", "axial", "rad"),
            P(None, "azim", "axial", "rad"),
            P("azim", "axial", "rad"),
            P(),
            P(),
            P(),
        ),
        out_specs=P(None, None, "azim", "axial", "rad"),
        check_vma=False,
    )
```

```python
import functools

import jax
import jax.numpy as jnp
from jax import lax
from jax.experimental import pallas as pl
from jax.experimental.pallas import tpu as pltpu
from jax.sharding import PartitionSpec as P

supersat_scale = 1.5
crowding = 0.02
MESH = pl.DeviceIdType.MESH
F32 = jnp.float32
CHUNKS = 3
HOLD = 1
EARLY = 2
EARLY_TWO = 2
HOLD2 = 3
REMOTE = 6 * CHUNKS + 6


def shifted(axis, step):
    size = lax.axis_size(axis)
    return {axis: lax.rem(lax.axis_index(axis) + step + size, size)}


def kernel(
    far_ref, af_ref, sm_ref, ss_ref, speeds_ref, flags_ref, zones_ref, growth_ref, transfer_ref, nucl_ref,
    out_ref,
    a_v, b_v, sm_v, ss_v, sp_v, fl_v, zn_v, g_s, t_s, n_s,
    pz_src, pz_dst, pa_src, pa_dst,
    az_src, az_one, az_two,
    ax_src1, ax_dst1, ax_src2, ax_dst2,
    rd_src1, rd_dst1, rd_src2, rd_dst2,
    local_sem, send_sem, recv_sem,
):
    sections = sm_ref.shape[1]
    above, below = shifted("azim", 1), shifted("azim", -1)
    right, left = shifted("rad", 1), shifted("rad", -1)
    other = shifted("axial", 1)
    first_half = lax.axis_index("axial") == 0

    size = sections // CHUNKS
    chunks = [pl.ds(c * size, size) for c in reversed(range(CHUNKS))]

    def sweep(step, init, chunk=None):
        if chunk is None:
            for chunk in chunks:
                init = sweep(step, init, chunk)
            return init
        top = chunk.start + chunk.size - 1
        return lax.fori_loop(0, chunk.size, lambda i, c: step(top - i, c), init, unroll=chunk.size)

    sent, held = [], []
    place = lax.rem(lax.axis_index("azim"), 4)

    def remote(src, dst, device, hold=None):
        n = len(sent)
        copy = pltpu.make_async_remote_copy(
            src_ref=src, dst_ref=dst, send_sem=send_sem.at[n], recv_sem=recv_sem.at[n],
            device_id=device, device_id_type=MESH,
        )
        if hold is None:
            copy.start()
        else:
            pl.when(jnp.logical_not(hold))(copy.start)
            held.append((hold, copy))
        sent.append(copy)
        return copy

    loads = [
        pltpu.make_async_copy(src, dst, local_sem.at[n])
        for n, (src, dst) in enumerate([
            (speeds_ref, sp_v), (flags_ref, fl_v), (af_ref, a_v.at[:, 0:sections]),
            (zones_ref, zn_v), (growth_ref, g_s), (transfer_ref, t_s), (nucl_ref, n_s),
            (sm_ref, sm_v), (ss_ref, ss_v),
        ])
    ]
    barrier = pltpu.get_barrier_semaphore()
    for device in (above, below, right, left, other):
        pl.semaphore_signal(barrier, inc=1, device_id=device, device_id_type=MESH)
    for copy in loads:
        copy.start()
    pl.semaphore_wait(barrier, 5)

    planes1 = [
        (
            remote(far_ref.at[:, c, 1], az_one.at[:, c, 0], above, place == 1),
            remote(far_ref.at[:, c, 0], az_one.at[:, c, 1], below, place == 2),
        )
        for c in chunks
    ]

    row = lax.broadcasted_iota(jnp.int32, (8, 128), 0)
    lane = lax.broadcasted_iota(jnp.int32, (8, 128), 1)
    arow = lax.rem(row, 4)
    edge = jnp.where(first_half, 3, 0)

    def pack_axial(values):
        packed = values[0]
        for k in range(1, 4):
            packed = jnp.where(arow == lax.rem(edge + k, 4), pltpu.roll(values[k], k, 0), packed)
        return packed

    def pack_radial(s, values, packs):
        here = lax.shift_right_logical(lane, 1) == s
        return [jnp.where(here, pltpu.roll(x, 2 * s + 1, 1), pack) for x, pack in zip(values, packs)]

    zero = jnp.zeros((8, 128), F32)

    loads[0].wait()
    loads[1].wait()
    upwind = fl_v[...].astype(F32)
    speeds = sp_v[...]
    p = speeds * upwind
    q = speeds * (1.0 - upwind)
    pz_src[...] = p[0]
    pa_src[...] = p[1]
    rd_src1[4] = p[2]
    pz = remote(pz_src, pz_dst, below)
    pa = remote(pa_src, pa_dst, other)

    loads[2].wait()
    a_v[:, sections] = jnp.zeros((4, 8, 128), F32)
    b_v[:, sections] = jnp.zeros((4, 8, 128), F32)

    def pack_first(s, packs):
        values = [a_v[k, s] for k in range(4)]
        ax_src1[s] = pack_axial(values)
        return pack_radial(s, values, packs)

    packs, rows1 = [zero] * 4, []
    for c in chunks:
        packs = sweep(pack_first, packs, c)
        rows1.append(remote(ax_src1.at[c], ax_dst1.at[c], other))
    for k in range(4):
        rd_src1[k] = packs[k]
    lanes1 = (
        remote(rd_src1, rd_dst1.at[0], right),
        remote(rd_src1, rd_dst1.at[1], left),
    )

    waits = rows1[:HOLD]
    late = (place == 1) | (place == 2)

    @pl.when(late)
    def _():
        for copy in waits:
            copy.wait_send()

    for hold, copy in held:
        pl.when(hold)(copy.start)

    for copy in loads[3:7]:
        copy.wait()
    zones = zn_v[...]
    nucleation = zero
    for z in range(nucl_ref.shape[0]):
        nucleation = nucleation + jnp.where(zones == z, n_s[z], 0.0)
    loads[7].wait()

    def slope(s, k, values, after):
        t = t_s[s]
        term = t * (after - values[k])
        if k < 3:
            term = term + ((k + 1) * g_s[s]) * values[k + 1]
        return term

    def source_sums(s, values, after, state, sums):
        gain, third = sums
        for k in range(4):
            u = state[k, s].astype(F32)
            gain = gain + u * slope(s, k, values, after[k])
            if k == 3:
                third = third + u * u
        return gain, third

    def source_scalars(sums, first):
        gain, third = sums
        sigma = supersat_scale / (1.0 + crowding * third)
        birth = first[0] + 0.5 * first[1] + 0.25 * first[2] + 0.125 * first[3]
        total = gain + 2.0 * sigma * nucleation * birth
        return sigma, (-2.0 * crowding / supersat_scale) * sigma * sigma * total

    def first_sums(s, sums):
        values = [a_v[k, s] for k in range(4)]
        after = [a_v[k, s + 1] for k in range(4)]
        return source_sums(s, values, after, sm_v, sums)

    sums = sweep(first_sums, (zero, zero))
    sigma1, third1 = source_scalars(sums, [a_v[k, 0] for k in range(4)])

    pa.wait_recv()
    for copy in lanes1:
        copy.wait_recv()
    p0, p1, p2 = p[0], p[1], p[2]
    q0, q1, q2 = q[0], q[1], q[2]
    c_mid = jnp.where(row < 4, pltpu.roll(p0, 4, 0), q0)
    c_up = jnp.where(arow < 3, pltpu.roll(p1, 7, 0), 0.0)
    c_low = jnp.where(arow > 0, q1, 0.0)
    far_face = jnp.where(first_half, pltpu.roll(pa_dst[...], 3, 0), 0.0)
    ax_all = jnp.where(arow == 0, q1, jnp.where(arow == 3, far_face, 0.0))
    ax_halo = jnp.where(arow == edge, ax_all, 0.0)
    c_right = jnp.where(lane < 127, pltpu.roll(p2, 127, 1), 0.0)
    c_left = jnp.where(lane > 0, q2, 0.0)
    rad_index = lax.axis_index("rad")
    rad_last = lax.axis_size("rad") - 1
    rd_high = jnp.where(rad_index < rad_last, pltpu.roll(rd_dst1[1, 4], 127, 1), 0.0)
    rd_all = jnp.where(lane == 0, q2, jnp.where(lane == 127, rd_high, 0.0))
    rd_halo = jnp.where((lane == 0) & (rad_index == 0), 0.0, rd_all)
    diagonal = c_mid + c_up + c_low + ax_all + c_right + c_left + rd_all

    def radial_halos(dst):
        even = lax.rem(lane, 2) == 0
        return [jnp.where(even, dst[0, k], pltpu.roll(dst[1, k], 126, 1)) for k in range(4)]

    def axial_halo(packed):
        return jnp.where(first_half, pltpu.roll(packed, 3, 0), pltpu.roll(packed, 5, 0))

    def row_halo(k, axial):
        return axial if k == 0 else pltpu.roll(axial, 8 - k, 0)

    def radial_halo(s, k, radial):
        return pltpu.roll(radial[k], lax.rem(128 - 2 * s, 128), 1)

    def inside(x, mid, up, low, right_c, left_c):
        return (
            mid * pltpu.roll(x, 4, 0)
            + up * pltpu.roll(x, 7, 0)
            + low * pltpu.roll(x, 1, 0)
            + right_c * pltpu.roll(x, 127, 1)
            + left_c * pltpu.roll(x, 1, 1)
        )

    radial1 = radial_halos(rd_dst1)
    keep1 = 0.5 * (1.0 - diagonal)
    half = [0.5 * c for c in (c_mid, c_up, c_low, c_right, c_left)]
    half_ax, half_rd = 0.5 * ax_halo, 0.5 * rd_halo
    half_sigma, half_third = 0.5 * sigma1, 0.5 * third1

    def first_stage(s, carry):
        values = [a_v[k, s] for k in range(4)]
        axial = axial_halo(ax_dst1[s])
        for k in range(4):
            x = values[k]
            ax, rd = row_halo(k, axial), radial_halo(s, k, radial1)
            y = keep1 * x + inside(x, *half) + half_ax * ax + half_rd * rd
            y = y + half_sigma * slope(s, k, values, a_v[k, s + 1])
            if k == 3:
                y = y + half_third * sm_v[3, s].astype(F32)
            b_v[k, s] = y
            az_src[0, k, s] = y[0:4]
            az_src[1, k, s] = y[4:8]
        return carry

    planes2 = []
    held.clear()

    def later(chunk, one_link, two_links):
        n = [chunk is c for c in chunks].index(True)
        hold = [place == p for p, early in ((one_link, EARLY), (two_links, EARLY_TWO)) if n >= early]
        return functools.reduce(jnp.logical_or, hold) if hold else None

    for c, rows in zip(chunks, rows1):
        rows.wait_recv()
        sweep(first_stage, 0, c)
        planes2.append((
            remote(az_src.at[1, :, c], az_two.at[:, c, 0], above, later(c, 1, 3)),
            remote(az_src.at[0, :, c], az_two.at[:, c, 1], below, later(c, 2, 0)),
        ))

    pz.wait_recv()
    az_halo = jnp.where(row < 4, q0, pltpu.roll(pz_dst[...], 4, 0))
    half_az = 0.5 * az_halo
    loads[8].wait()

    def halo_planes(ref, k, s):
        return jnp.concatenate([ref[k, s, 0], ref[k, s, 1]], axis=0)

    def middle_stage(s, carry):
        packs, after, sums = carry
        values = []
        for k in range(4):
            y = b_v[k, s] + half_az * (halo_planes(az_one, k, s) - a_v[k, s])
            b_v[k, s] = y
            values.append(y)
        ax_src2[s] = pack_axial(values)
        packs = pack_radial(s, values, packs)
        sums = source_sums(s, values, after, ss_v, sums)
        return packs, values, sums

    carry, rows2 = ([zero] * 4, [zero] * 4, (zero, zero)), []
    for c, planes in zip(chunks, planes1):
        for copy in planes:
            copy.wait_recv()
        carry = sweep(middle_stage, carry, c)
        rows2.append(remote(ax_src2.at[c], ax_dst2.at[c], other))
    packs, head, sums = carry
    for k in range(4):
        rd_src2[k] = packs[k]
    lanes2 = (
        remote(rd_src2, rd_dst2.at[0], right),
        remote(rd_src2, rd_dst2.at[1], left),
    )
    sigma2, third2 = source_scalars(sums, head)
    keep2 = 1.0 - (diagonal + az_halo)

    def second_stage(s, carry):
        values = [b_v[k, s] for k in range(4)]
        for k in range(4):
            x = values[k]
            y = keep2 * x + 0.5 * a_v[k, s] + inside(x, c_mid, c_up, c_low, c_right, c_left)
            y = y + sigma2 * slope(s, k, values, b_v[k, s + 1])
            if k == 3:
                y = y + third2 * ss_v[3, s].astype(F32)
            out_ref[k, s] = y
        return carry

    sweep(second_stage, 0)
    for copy in lanes2:
        copy.wait_recv()
    radial2 = radial_halos(rd_dst2)

    def add_lanes(s, carry):
        for k in range(4):
            out_ref[k, s] = out_ref[k, s] + rd_halo * radial_halo(s, k, radial2)
        return carry

    def add_planes(s, carry):
        for k in range(4):
            out_ref[k, s] = out_ref[k, s] + az_halo * halo_planes(az_two, k, s)
        return carry

    def add_rows(s, carry):
        axial = axial_halo(ax_dst2[s])
        for k in range(4):
            out_ref[k, s] = out_ref[k, s] + ax_halo * row_halo(k, axial)
        return carry

    sweep(add_lanes, 0)

    for copy in rows2[:HOLD2]:
        copy.wait_send()
    for hold, copy in held:
        pl.when(hold)(copy.start)

    for c, planes, rows in zip(chunks, planes2, rows2):
        for copy in planes:
            copy.wait_recv()
        sweep(add_planes, 0, c)
        rows.wait_recv()
        sweep(add_rows, 0, c)
    for copy in sent:
        if any(copy is w for w in rows2[:HOLD2]):
            continue
        if any(copy is w for w in waits):
            pl.when(jnp.logical_not(late))(copy.wait_send)
        else:
            copy.wait_send()


def shards(
    adjoint_final,
    state_start,
    state_middle,
    speeds,
    flags,
    zones,
    growth_rate,
    transfer_rate,
    nucleation_rate,
):
    dims = adjoint_final.shape
    moms, sections = dims[0], dims[1]
    flat = (moms, sections, 8, 128)
    hbm = pl.BlockSpec(memory_space=pltpu.MemorySpace.HBM)
    vmem = pltpu.VMEM
    dma = pltpu.SemaphoreType.DMA
    out = pl.pallas_call(
        kernel,
        out_shape=jax.ShapeDtypeStruct(flat, F32),
        in_specs=[hbm] * 10,
        out_specs=pl.BlockSpec(memory_space=pltpu.VMEM),
        scratch_shapes=[
            vmem((moms, sections + 1, 8, 128), F32),
            vmem((moms, sections + 1, 8, 128), F32),
            vmem(flat, jnp.bfloat16),
            vmem(flat, jnp.bfloat16),
            vmem((3, 8, 128), F32),
            vmem((3, 8, 128), jnp.int32),
            vmem((8, 128), jnp.int32),
            pltpu.SMEM(growth_rate.shape, F32),
            pltpu.SMEM(transfer_rate.shape, F32),
            pltpu.SMEM(nucleation_rate.shape, F32),
            vmem((8, 128), F32),
            vmem((8, 128), F32),
            vmem((8, 128), F32),
            vmem((8, 128), F32),
            vmem((2, moms, sections, 4, 128), F32),
            vmem((moms, sections, 2, 4, 128), F32),
            vmem((moms, sections, 2, 4, 128), F32),
            vmem((sections, 8, 128), F32),
            vmem((sections, 8, 128), F32),
            vmem((sections, 8, 128), F32),
            vmem((sections, 8, 128), F32),
            vmem((5, 8, 128), F32),
            vmem((2, 5, 8, 128), F32),
            vmem((4, 8, 128), F32),
            vmem((2, 4, 8, 128), F32),
            dma((9,)),
            dma((REMOTE,)),
            dma((REMOTE,)),
        ],
        compiler_params=pltpu.CompilerParams(
            collective_id=0, has_side_effects=True, vmem_limit_bytes=40 << 20
        ),
    )(*[
        pltpu.with_memory_space_constraint(x, pltpu.MemorySpace.HBM)
        for x in (
            adjoint_final,
            adjoint_final.reshape(flat),
            state_middle.reshape(flat),
            state_start.reshape(flat),
            speeds.reshape(3, 8, 128),
            flags.reshape(3, 8, 128),
            zones.reshape(8, 128),
            growth_rate,
            transfer_rate,
            nucleation_rate,
        )
    ])
    return out.reshape(dims)


def solution(mesh):
    return jax.shard_map(
        shards,
        mesh=mesh,
        in_specs=(
            P(None, None, "azim", "axial", "rad"),
            P(None, None, "azim", "axial", "rad"),
            P(None, None, "azim", "axial", "rad"),
            P(None, "azim", "axial", "rad"),
            P(None, "azim", "axial", "rad"),
            P("azim", "axial", "rad"),
            P(),
            P(),
            P(),
        ),
        out_specs=P(None, None, "azim", "axial", "rad"),
        check_vma=False,
    )
```

```python
import functools

import jax
import jax.numpy as jnp
from jax import lax
from jax.experimental import pallas as pl
from jax.experimental.pallas import tpu as pltpu
from jax.sharding import PartitionSpec as P

supersat_scale = 1.5
crowding = 0.02
MESH = pl.DeviceIdType.MESH
F32 = jnp.float32
CHUNKS = 3
HOLD = 1
EARLY = 2
EARLY_TWO = 2
HOLD2 = 2
REMOTE = 6 * CHUNKS + 6


def shifted(axis, step):
    size = lax.axis_size(axis)
    return {axis: lax.rem(lax.axis_index(axis) + step + size, size)}


def kernel(
    far_ref, af_ref, sm_ref, ss_ref, speeds_ref, flags_ref, zones_ref, growth_ref, transfer_ref, nucl_ref,
    out_ref,
    a_v, b_v, sm_v, ss_v, sp_v, fl_v, zn_v, g_s, t_s, n_s,
    pz_src, pz_dst, pa_src, pa_dst,
    az_src, az_one, az_two,
    ax_src1, ax_dst1, ax_src2, ax_dst2,
    rd_src1, rd_dst1, rd_src2, rd_dst2,
    local_sem, send_sem, recv_sem,
):
    sections = sm_ref.shape[1]
    above, below = shifted("azim", 1), shifted("azim", -1)
    right, left = shifted("rad", 1), shifted("rad", -1)
    other = shifted("axial", 1)
    first_half = lax.axis_index("axial") == 0

    size = sections // CHUNKS
    chunks = [pl.ds(c * size, size) for c in reversed(range(CHUNKS))]

    def sweep(step, init, chunk=None):
        if chunk is None:
            for chunk in chunks:
                init = sweep(step, init, chunk)
            return init
        top = chunk.start + chunk.size - 1
        return lax.fori_loop(0, chunk.size, lambda i, c: step(top - i, c), init, unroll=chunk.size)

    sent, held = [], []
    place = lax.rem(lax.axis_index("azim"), 4)

    def remote(src, dst, device, hold=None):
        n = len(sent)
        copy = pltpu.make_async_remote_copy(
            src_ref=src, dst_ref=dst, send_sem=send_sem.at[n], recv_sem=recv_sem.at[n],
            device_id=device, device_id_type=MESH,
        )
        if hold is None:
            copy.start()
        else:
            pl.when(jnp.logical_not(hold))(copy.start)
            held.append((hold, copy))
        sent.append(copy)
        return copy

    loads = [
        pltpu.make_async_copy(src, dst, local_sem.at[n])
        for n, (src, dst) in enumerate([
            (speeds_ref, sp_v), (flags_ref, fl_v), (af_ref, a_v.at[:, 0:sections]),
            (zones_ref, zn_v), (growth_ref, g_s), (transfer_ref, t_s), (nucl_ref, n_s),
            (sm_ref, sm_v), (ss_ref, ss_v),
        ])
    ]
    barrier = pltpu.get_barrier_semaphore()
    for device in (above, below, right, left, other):
        pl.semaphore_signal(barrier, inc=1, device_id=device, device_id_type=MESH)
    for copy in loads:
        copy.start()
    pl.semaphore_wait(barrier, 5)

    planes1 = [
        (
            remote(far_ref.at[:, c, 1], az_one.at[:, c, 0], above, place == 1),
            remote(far_ref.at[:, c, 0], az_one.at[:, c, 1], below, place == 2),
        )
        for c in chunks
    ]

    row = lax.broadcasted_iota(jnp.int32, (8, 128), 0)
    lane = lax.broadcasted_iota(jnp.int32, (8, 128), 1)
    arow = lax.rem(row, 4)
    edge = jnp.where(first_half, 3, 0)

    def pack_axial(values):
        packed = values[0]
        for k in range(1, 4):
            packed = jnp.where(arow == lax.rem(edge + k, 4), pltpu.roll(values[k], k, 0), packed)
        return packed

    def pack_radial(s, values, packs):
        here = lax.shift_right_logical(lane, 1) == s
        return [jnp.where(here, pltpu.roll(x, 2 * s + 1, 1), pack) for x, pack in zip(values, packs)]

    zero = jnp.zeros((8, 128), F32)

    loads[0].wait()
    loads[1].wait()
    upwind = fl_v[...].astype(F32)
    speeds = sp_v[...]
    p = speeds * upwind
    q = speeds * (1.0 - upwind)
    pz_src[...] = p[0]
    pa_src[...] = p[1]
    rd_src1[4] = p[2]
    pz = remote(pz_src, pz_dst, below)
    pa = remote(pa_src, pa_dst, other)

    loads[2].wait()
    a_v[:, sections] = jnp.zeros((4, 8, 128), F32)
    b_v[:, sections] = jnp.zeros((4, 8, 128), F32)

    def pack_first(s, packs):
        values = [a_v[k, s] for k in range(4)]
        ax_src1[s] = pack_axial(values)
        return pack_radial(s, values, packs)

    packs, rows1 = [zero] * 4, []
    for c in chunks:
        packs = sweep(pack_first, packs, c)
        rows1.append(remote(ax_src1.at[c], ax_dst1.at[c], other))
    for k in range(4):
        rd_src1[k] = packs[k]
    lanes1 = (
        remote(rd_src1, rd_dst1.at[0], right),
        remote(rd_src1, rd_dst1.at[1], left),
    )

    waits = rows1[:HOLD]
    late = (place == 1) | (place == 2)

    @pl.when(late)
    def _():
        for copy in waits:
            copy.wait_send()

    for hold, copy in held:
        pl.when(hold)(copy.start)

    for copy in loads[3:7]:
        copy.wait()
    zones = zn_v[...]
    nucleation = zero
    for z in range(nucl_ref.shape[0]):
        nucleation = nucleation + jnp.where(zones == z, n_s[z], 0.0)
    loads[7].wait()

    def slope(s, k, values, after):
        t = t_s[s]
        term = t * (after - values[k])
        if k < 3:
            term = term + ((k + 1) * g_s[s]) * values[k + 1]
        return term

    def source_sums(s, values, after, state, sums):
        gain, third = sums
        for k in range(4):
            u = state[k, s].astype(F32)
            gain = gain + u * slope(s, k, values, after[k])
            if k == 3:
                third = third + u * u
        return gain, third

    def source_scalars(sums, first):
        gain, third = sums
        sigma = supersat_scale / (1.0 + crowding * third)
        birth = first[0] + 0.5 * first[1] + 0.25 * first[2] + 0.125 * first[3]
        total = gain + 2.0 * sigma * nucleation * birth
        return sigma, (-2.0 * crowding / supersat_scale) * sigma * sigma * total

    def first_sums(s, sums):
        values = [a_v[k, s] for k in range(4)]
        after = [a_v[k, s + 1] for k in range(4)]
        return source_sums(s, values, after, sm_v, sums)

    sums = sweep(first_sums, (zero, zero))
    sigma1, third1 = source_scalars(sums, [a_v[k, 0] for k in range(4)])

    pa.wait_recv()
    for copy in lanes1:
        copy.wait_recv()
    p0, p1, p2 = p[0], p[1], p[2]
    q0, q1, q2 = q[0], q[1], q[2]
    c_mid = jnp.where(row < 4, pltpu.roll(p0, 4, 0), q0)
    c_up = jnp.where(arow < 3, pltpu.roll(p1, 7, 0), 0.0)
    c_low = jnp.where(arow > 0, q1, 0.0)
    far_face = jnp.where(first_half, pltpu.roll(pa_dst[...], 3, 0), 0.0)
    ax_all = jnp.where(arow == 0, q1, jnp.where(arow == 3, far_face, 0.0))
    ax_halo = jnp.where(arow == edge, ax_all, 0.0)
    c_right = jnp.where(lane < 127, pltpu.roll(p2, 127, 1), 0.0)
    c_left = jnp.where(lane > 0, q2, 0.0)
    rad_index = lax.axis_index("rad")
    rad_last = lax.axis_size("rad") - 1
    rd_high = jnp.where(rad_index < rad_last, pltpu.roll(rd_dst1[1, 4], 127, 1), 0.0)
    rd_all = jnp.where(lane == 0, q2, jnp.where(lane == 127, rd_high, 0.0))
    rd_halo = jnp.where((lane == 0) & (rad_index == 0), 0.0, rd_all)
    diagonal = c_mid + c_up + c_low + ax_all + c_right + c_left + rd_all

    def radial_halos(dst):
        even = lax.rem(lane, 2) == 0
        return [jnp.where(even, dst[0, k], pltpu.roll(dst[1, k], 126, 1)) for k in range(4)]

    def axial_halo(packed):
        return jnp.where(first_half, pltpu.roll(packed, 3, 0), pltpu.roll(packed, 5, 0))

    def row_halo(k, axial):
        return axial if k == 0 else pltpu.roll(axial, 8 - k, 0)

    def radial_halo(s, k, radial):
        return pltpu.roll(radial[k], lax.rem(128 - 2 * s, 128), 1)

    def inside(x, mid, up, low, right_c, left_c):
        return (
            mid * pltpu.roll(x, 4, 0)
            + up * pltpu.roll(x, 7, 0)
            + low * pltpu.roll(x, 1, 0)
            + right_c * pltpu.roll(x, 127, 1)
            + left_c * pltpu.roll(x, 1, 1)
        )

    radial1 = radial_halos(rd_dst1)
    keep1 = 0.5 * (1.0 - diagonal)
    half = [0.5 * c for c in (c_mid, c_up, c_low, c_right, c_left)]
    half_ax, half_rd = 0.5 * ax_halo, 0.5 * rd_halo
    half_sigma, half_third = 0.5 * sigma1, 0.5 * third1

    def first_stage(s, carry):
        values = [a_v[k, s] for k in range(4)]
        axial = axial_halo(ax_dst1[s])
        for k in range(4):
            x = values[k]
            ax, rd = row_halo(k, axial), radial_halo(s, k, radial1)
            y = keep1 * x + inside(x, *half) + half_ax * ax + half_rd * rd
            y = y + half_sigma * slope(s, k, values, a_v[k, s + 1])
            if k == 3:
                y = y + half_third * sm_v[3, s].astype(F32)
            b_v[k, s] = y
            az_src[0, k, s] = y[0:4]
            az_src[1, k, s] = y[4:8]
        return carry

    planes2 = []
    held.clear()

    def later(chunk, one_link, two_links):
        n = [chunk is c for c in chunks].index(True)
        hold = [place == p for p, early in ((one_link, EARLY), (two_links, EARLY_TWO)) if n >= early]
        return functools.reduce(jnp.logical_or, hold) if hold else None

    for c, rows in zip(chunks, rows1):
        rows.wait_recv()
        sweep(first_stage, 0, c)
        planes2.append((
            remote(az_src.at[1, :, c], az_two.at[:, c, 0], above, later(c, 1, 3)),
            remote(az_src.at[0, :, c], az_two.at[:, c, 1], below, later(c, 2, 0)),
        ))

    pz.wait_recv()
    az_halo = jnp.where(row < 4, q0, pltpu.roll(pz_dst[...], 4, 0))
    half_az = 0.5 * az_halo
    loads[8].wait()

    def halo_planes(ref, k, s):
        return jnp.concatenate([ref[k, s, 0], ref[k, s, 1]], axis=0)

    def middle_stage(s, carry):
        packs, after, sums = carry
        values = []
        for k in range(4):
            y = b_v[k, s] + half_az * (halo_planes(az_one, k, s) - a_v[k, s])
            b_v[k, s] = y
            values.append(y)
        ax_src2[s] = pack_axial(values)
        packs = pack_radial(s, values, packs)
        sums = source_sums(s, values, after, ss_v, sums)
        return packs, values, sums

    carry, rows2 = ([zero] * 4, [zero] * 4, (zero, zero)), []
    for c, planes in zip(chunks, planes1):
        for copy in planes:
            copy.wait_recv()
        carry = sweep(middle_stage, carry, c)
        rows2.append(remote(ax_src2.at[c], ax_dst2.at[c], other))
    packs, head, sums = carry
    for k in range(4):
        rd_src2[k] = packs[k]
    lanes2 = (
        remote(rd_src2, rd_dst2.at[0], right),
        remote(rd_src2, rd_dst2.at[1], left),
    )
    sigma2, third2 = source_scalars(sums, head)
    keep2 = 1.0 - (diagonal + az_halo)

    def second_stage(s, carry):
        values = [b_v[k, s] for k in range(4)]
        for k in range(4):
            x = values[k]
            y = keep2 * x + 0.5 * a_v[k, s] + inside(x, c_mid, c_up, c_low, c_right, c_left)
            y = y + sigma2 * slope(s, k, values, b_v[k, s + 1])
            if k == 3:
                y = y + third2 * ss_v[3, s].astype(F32)
            out_ref[k, s] = y
        return carry

    sweep(second_stage, 0)
    for copy in lanes2:
        copy.wait_recv()
    radial2 = radial_halos(rd_dst2)

    def add_lanes(s, carry):
        for k in range(4):
            out_ref[k, s] = out_ref[k, s] + rd_halo * radial_halo(s, k, radial2)
        return carry

    def add_planes(s, carry):
        for k in range(4):
            out_ref[k, s] = out_ref[k, s] + az_halo * halo_planes(az_two, k, s)
        return carry

    def add_rows(s, carry):
        axial = axial_halo(ax_dst2[s])
        for k in range(4):
            out_ref[k, s] = out_ref[k, s] + ax_halo * row_halo(k, axial)
        return carry

    sweep(add_lanes, 0)

    for copy in rows2[:HOLD2]:
        copy.wait_send()
    for hold, copy in held:
        pl.when(hold)(copy.start)

    for c, planes, rows in zip(chunks, planes2, rows2):
        for copy in planes:
            copy.wait_recv()
        sweep(add_planes, 0, c)
        rows.wait_recv()
        sweep(add_rows, 0, c)
    for copy in sent:
        if any(copy is w for w in rows2[:HOLD2]):
            continue
        if any(copy is w for w in waits):
            pl.when(jnp.logical_not(late))(copy.wait_send)
        else:
            copy.wait_send()


def shards(
    adjoint_final,
    state_start,
    state_middle,
    speeds,
    flags,
    zones,
    growth_rate,
    transfer_rate,
    nucleation_rate,
):
    dims = adjoint_final.shape
    moms, sections = dims[0], dims[1]
    flat = (moms, sections, 8, 128)
    hbm = pl.BlockSpec(memory_space=pltpu.MemorySpace.HBM)
    vmem = pltpu.VMEM
    dma = pltpu.SemaphoreType.DMA
    out = pl.pallas_call(
        kernel,
        out_shape=jax.ShapeDtypeStruct(flat, F32),
        in_specs=[hbm] * 10,
        out_specs=pl.BlockSpec(memory_space=pltpu.VMEM),
        scratch_shapes=[
            vmem((moms, sections + 1, 8, 128), F32),
            vmem((moms, sections + 1, 8, 128), F32),
            vmem(flat, jnp.bfloat16),
            vmem(flat, jnp.bfloat16),
            vmem((3, 8, 128), F32),
            vmem((3, 8, 128), jnp.int32),
            vmem((8, 128), jnp.int32),
            pltpu.SMEM(growth_rate.shape, F32),
            pltpu.SMEM(transfer_rate.shape, F32),
            pltpu.SMEM(nucleation_rate.shape, F32),
            vmem((8, 128), F32),
            vmem((8, 128), F32),
            vmem((8, 128), F32),
            vmem((8, 128), F32),
            vmem((2, moms, sections, 4, 128), F32),
            vmem((moms, sections, 2, 4, 128), F32),
            vmem((moms, sections, 2, 4, 128), F32),
            vmem((sections, 8, 128), F32),
            vmem((sections, 8, 128), F32),
            vmem((sections, 8, 128), F32),
            vmem((sections, 8, 128), F32),
            vmem((5, 8, 128), F32),
            vmem((2, 5, 8, 128), F32),
            vmem((4, 8, 128), F32),
            vmem((2, 4, 8, 128), F32),
            dma((9,)),
            dma((REMOTE,)),
            dma((REMOTE,)),
        ],
        compiler_params=pltpu.CompilerParams(
            collective_id=0, has_side_effects=True, vmem_limit_bytes=40 << 20
        ),
    )(*[
        pltpu.with_memory_space_constraint(x, pltpu.MemorySpace.HBM)
        for x in (
            adjoint_final,
            adjoint_final.reshape(flat),
            state_middle.reshape(flat),
            state_start.reshape(flat),
            speeds.reshape(3, 8, 128),
            flags.reshape(3, 8, 128),
            zones.reshape(8, 128),
            growth_rate,
            transfer_rate,
            nucleation_rate,
        )
    ])
    return out.reshape(dims)


def solution(mesh):
    return jax.shard_map(
        shards,
        mesh=mesh,
        in_specs=(
            P(None, None, "azim", "axial", "rad"),
            P(None, None, "azim", "axial", "rad"),
            P(None, None, "azim", "axial", "rad"),
            P(None, "azim", "axial", "rad"),
            P(None, "azim", "axial", "rad"),
            P("azim", "axial", "rad"),
            P(),
            P(),
            P(),
        ),
        out_specs=P(None, None, "azim", "axial", "rad"),
        check_vma=False,
    )
```

```python
import functools

import jax
import jax.numpy as jnp
from jax import lax
from jax.experimental import pallas as pl
from jax.experimental.pallas import tpu as pltpu
from jax.sharding import PartitionSpec as P

supersat_scale = 1.5
crowding = 0.02
MESH = pl.DeviceIdType.MESH
F32 = jnp.float32
CHUNKS = 3
HOLD = 1
EARLY = 2
EARLY_TWO = 2
HOLD2 = 2
REMOTE = 6 * CHUNKS + 6


def shifted(axis, step):
    size = lax.axis_size(axis)
    return {axis: lax.rem(lax.axis_index(axis) + step + size, size)}


def kernel(
    far_ref, af_ref, sm_ref, ss_ref, speeds_ref, flags_ref, zones_ref, growth_ref, transfer_ref, nucl_ref,
    out_ref,
    a_v, b_v, sm_v, ss_v, sp_v, fl_v, zn_v, g_s, t_s, n_s,
    pz_src, pz_dst, pa_src, pa_dst,
    az_src, az_one, az_two,
    ax_src1, ax_dst1, ax_src2, ax_dst2,
    rd_src1, rd_dst1, rd_src2, rd_dst2,
    local_sem, send_sem, recv_sem,
):
    sections = sm_ref.shape[1]
    above, below = shifted("azim", 1), shifted("azim", -1)
    right, left = shifted("rad", 1), shifted("rad", -1)
    other = shifted("axial", 1)
    first_half = lax.axis_index("axial") == 0

    size = sections // CHUNKS
    chunks = [pl.ds(c * size, size) for c in reversed(range(CHUNKS))]

    def sweep(step, init, chunk=None):
        if chunk is None:
            for chunk in chunks:
                init = sweep(step, init, chunk)
            return init
        top = chunk.start + chunk.size - 1
        return lax.fori_loop(0, chunk.size, lambda i, c: step(top - i, c), init, unroll=chunk.size)

    sent, held = [], []
    place = lax.rem(lax.axis_index("azim"), 4)

    def remote(src, dst, device, hold=None):
        n = len(sent)
        copy = pltpu.make_async_remote_copy(
            src_ref=src, dst_ref=dst, send_sem=send_sem.at[n], recv_sem=recv_sem.at[n],
            device_id=device, device_id_type=MESH,
        )
        if hold is None:
            copy.start()
        else:
            pl.when(jnp.logical_not(hold))(copy.start)
            held.append((hold, copy))
        sent.append(copy)
        return copy

    loads = [
        pltpu.make_async_copy(src, dst, local_sem.at[n])
        for n, (src, dst) in enumerate([
            (speeds_ref, sp_v), (flags_ref, fl_v), (af_ref, a_v.at[:, 0:sections]),
            (zones_ref, zn_v), (growth_ref, g_s), (transfer_ref, t_s), (nucl_ref, n_s),
            (sm_ref, sm_v), (ss_ref, ss_v),
        ])
    ]
    barrier = pltpu.get_barrier_semaphore()
    for device in (other, above, below, right, left):
        pl.semaphore_signal(barrier, inc=1, device_id=device, device_id_type=MESH)
    for copy in loads:
        copy.start()
    pl.semaphore_wait(barrier, 5)

    planes1 = [
        (
            remote(far_ref.at[:, c, 1], az_one.at[:, c, 0], above, place == 1),
            remote(far_ref.at[:, c, 0], az_one.at[:, c, 1], below, place == 2),
        )
        for c in chunks
    ]

    row = lax.broadcasted_iota(jnp.int32, (8, 128), 0)
    lane = lax.broadcasted_iota(jnp.int32, (8, 128), 1)
    arow = lax.rem(row, 4)
    edge = jnp.where(first_half, 3, 0)

    def pack_axial(values):
        packed = values[0]
        for k in range(1, 4):
            packed = jnp.where(arow == lax.rem(edge + k, 4), pltpu.roll(values[k], k, 0), packed)
        return packed

    def pack_radial(s, values, packs):
        here = lax.shift_right_logical(lane, 1) == s
        return [jnp.where(here, pltpu.roll(x, 2 * s + 1, 1), pack) for x, pack in zip(values, packs)]

    zero = jnp.zeros((8, 128), F32)

    loads[0].wait()
    loads[1].wait()
    upwind = fl_v[...].astype(F32)
    speeds = sp_v[...]
    p = speeds * upwind
    q = speeds * (1.0 - upwind)
    pz_src[...] = p[0]
    pa_src[...] = p[1]
    rd_src1[4] = p[2]
    pz = remote(pz_src, pz_dst, below)
    pa = remote(pa_src, pa_dst, other)

    loads[2].wait()
    a_v[:, sections] = jnp.zeros((4, 8, 128), F32)
    b_v[:, sections] = jnp.zeros((4, 8, 128), F32)

    def pack_first(s, packs):
        values = [a_v[k, s] for k in range(4)]
        ax_src1[s] = pack_axial(values)
        return pack_radial(s, values, packs)

    packs, rows1 = [zero] * 4, []
    for c in chunks:
        packs = sweep(pack_first, packs, c)
        rows1.append(remote(ax_src1.at[c], ax_dst1.at[c], other))
    for k in range(4):
        rd_src1[k] = packs[k]
    lanes1 = (
        remote(rd_src1, rd_dst1.at[0], right),
        remote(rd_src1, rd_dst1.at[1], left),
    )

    waits = rows1[:HOLD]
    late = (place == 1) | (place == 2)

    @pl.when(late)
    def _():
        for copy in waits:
            copy.wait_send()

    for hold, copy in held:
        pl.when(hold)(copy.start)

    for copy in loads[3:7]:
        copy.wait()
    zones = zn_v[...]
    nucleation = zero
    for z in range(nucl_ref.shape[0]):
        nucleation = nucleation + jnp.where(zones == z, n_s[z], 0.0)
    loads[7].wait()

    def slope(s, k, values, after):
        t = t_s[s]
        term = t * (after - values[k])
        if k < 3:
            term = term + ((k + 1) * g_s[s]) * values[k + 1]
        return term

    def source_sums(s, values, after, state, sums):
        gain, third = sums
        for k in range(4):
            u = state[k, s].astype(F32)
            gain = gain + u * slope(s, k, values, after[k])
            if k == 3:
                third = third + u * u
        return gain, third

    def source_scalars(sums, first):
        gain, third = sums
        sigma = supersat_scale / (1.0 + crowding * third)
        birth = first[0] + 0.5 * first[1] + 0.25 * first[2] + 0.125 * first[3]
        total = gain + 2.0 * sigma * nucleation * birth
        return sigma, (-2.0 * crowding / supersat_scale) * sigma * sigma * total

    def first_sums(s, sums):
        values = [a_v[k, s] for k in range(4)]
        after = [a_v[k, s + 1] for k in range(4)]
        return source_sums(s, values, after, sm_v, sums)

    sums = sweep(first_sums, (zero, zero))
    sigma1, third1 = source_scalars(sums, [a_v[k, 0] for k in range(4)])

    pa.wait_recv()
    for copy in lanes1:
        copy.wait_recv()
    p0, p1, p2 = p[0], p[1], p[2]
    q0, q1, q2 = q[0], q[1], q[2]
    c_mid = jnp.where(row < 4, pltpu.roll(p0, 4, 0), q0)
    c_up = jnp.where(arow < 3, pltpu.roll(p1, 7, 0), 0.0)
    c_low = jnp.where(arow > 0, q1, 0.0)
    far_face = jnp.where(first_half, pltpu.roll(pa_dst[...], 3, 0), 0.0)
    ax_all = jnp.where(arow == 0, q1, jnp.where(arow == 3, far_face, 0.0))
    ax_halo = jnp.where(arow == edge, ax_all, 0.0)
    c_right = jnp.where(lane < 127, pltpu.roll(p2, 127, 1), 0.0)
    c_left = jnp.where(lane > 0, q2, 0.0)
    rad_index = lax.axis_index("rad")
    rad_last = lax.axis_size("rad") - 1
    rd_high = jnp.where(rad_index < rad_last, pltpu.roll(rd_dst1[1, 4], 127, 1), 0.0)
    rd_all = jnp.where(lane == 0, q2, jnp.where(lane == 127, rd_high, 0.0))
    rd_halo = jnp.where((lane == 0) & (rad_index == 0), 0.0, rd_all)
    diagonal = c_mid + c_up + c_low + ax_all + c_right + c_left + rd_all

    def radial_halos(dst):
        even = lax.rem(lane, 2) == 0
        return [jnp.where(even, dst[0, k], pltpu.roll(dst[1, k], 126, 1)) for k in range(4)]

    def axial_halo(packed):
        return jnp.where(first_half, pltpu.roll(packed, 3, 0), pltpu.roll(packed, 5, 0))

    def row_halo(k, axial):
        return axial if k == 0 else pltpu.roll(axial, 8 - k, 0)

    def radial_halo(s, k, radial):
        return pltpu.roll(radial[k], lax.rem(128 - 2 * s, 128), 1)

    def inside(x, mid, up, low, right_c, left_c):
        return (
            mid * pltpu.roll(x, 4, 0)
            + up * pltpu.roll(x, 7, 0)
            + low * pltpu.roll(x, 1, 0)
            + right_c * pltpu.roll(x, 127, 1)
            + left_c * pltpu.roll(x, 1, 1)
        )

    radial1 = radial_halos(rd_dst1)
    keep1 = 0.5 * (1.0 - diagonal)
    half = [0.5 * c for c in (c_mid, c_up, c_low, c_right, c_left)]
    half_ax, half_rd = 0.5 * ax_halo, 0.5 * rd_halo
    half_sigma, half_third = 0.5 * sigma1, 0.5 * third1

    def first_stage(s, carry):
        values = [a_v[k, s] for k in range(4)]
        axial = axial_halo(ax_dst1[s])
        for k in range(4):
            x = values[k]
            ax, rd = row_halo(k, axial), radial_halo(s, k, radial1)
            y = keep1 * x + inside(x, *half) + half_ax * ax + half_rd * rd
            y = y + half_sigma * slope(s, k, values, a_v[k, s + 1])
            if k == 3:
                y = y + half_third * sm_v[3, s].astype(F32)
            b_v[k, s] = y
            az_src[0, k, s] = y[0:4]
            az_src[1, k, s] = y[4:8]
        return carry

    planes2 = []
    held.clear()

    def later(chunk, one_link, two_links):
        n = [chunk is c for c in chunks].index(True)
        hold = [place == p for p, early in ((one_link, EARLY), (two_links, EARLY_TWO)) if n >= early]
        return functools.reduce(jnp.logical_or, hold) if hold else None

    for c, rows in zip(chunks, rows1):
        rows.wait_recv()
        sweep(first_stage, 0, c)
        planes2.append((
            remote(az_src.at[1, :, c], az_two.at[:, c, 0], above, later(c, 1, 3)),
            remote(az_src.at[0, :, c], az_two.at[:, c, 1], below, later(c, 2, 0)),
        ))

    pz.wait_recv()
    az_halo = jnp.where(row < 4, q0, pltpu.roll(pz_dst[...], 4, 0))
    half_az = 0.5 * az_halo
    loads[8].wait()

    def halo_planes(ref, k, s):
        return jnp.concatenate([ref[k, s, 0], ref[k, s, 1]], axis=0)

    def middle_stage(s, carry):
        packs, after, sums = carry
        values = []
        for k in range(4):
            y = b_v[k, s] + half_az * (halo_planes(az_one, k, s) - a_v[k, s])
            b_v[k, s] = y
            values.append(y)
        ax_src2[s] = pack_axial(values)
        packs = pack_radial(s, values, packs)
        sums = source_sums(s, values, after, ss_v, sums)
        return packs, values, sums

    carry, rows2 = ([zero] * 4, [zero] * 4, (zero, zero)), []
    for c, planes in zip(chunks, planes1):
        for copy in planes:
            copy.wait_recv()
        carry = sweep(middle_stage, carry, c)
        rows2.append(remote(ax_src2.at[c], ax_dst2.at[c], other))
    packs, head, sums = carry
    for k in range(4):
        rd_src2[k] = packs[k]
    lanes2 = (
        remote(rd_src2, rd_dst2.at[0], right),
        remote(rd_src2, rd_dst2.at[1], left),
    )
    sigma2, third2 = source_scalars(sums, head)
    keep2 = 1.0 - (diagonal + az_halo)

    def second_stage(s, carry):
        values = [b_v[k, s] for k in range(4)]
        for k in range(4):
            x = values[k]
            y = keep2 * x + 0.5 * a_v[k, s] + inside(x, c_mid, c_up, c_low, c_right, c_left)
            y = y + sigma2 * slope(s, k, values, b_v[k, s + 1])
            if k == 3:
                y = y + third2 * ss_v[3, s].astype(F32)
            out_ref[k, s] = y
        return carry

    sweep(second_stage, 0)
    for copy in lanes2:
        copy.wait_recv()
    radial2 = radial_halos(rd_dst2)

    def add_lanes(s, carry):
        for k in range(4):
            out_ref[k, s] = out_ref[k, s] + rd_halo * radial_halo(s, k, radial2)
        return carry

    def add_planes(s, carry):
        for k in range(4):
            out_ref[k, s] = out_ref[k, s] + az_halo * halo_planes(az_two, k, s)
        return carry

    def add_rows(s, carry):
        axial = axial_halo(ax_dst2[s])
        for k in range(4):
            out_ref[k, s] = out_ref[k, s] + ax_halo * row_halo(k, axial)
        return carry

    sweep(add_lanes, 0)

    for copy in rows2[:HOLD2]:
        copy.wait_send()
    for hold, copy in held:
        pl.when(hold)(copy.start)

    for c, planes, rows in zip(chunks, planes2, rows2):
        for copy in planes:
            copy.wait_recv()
        sweep(add_planes, 0, c)
        rows.wait_recv()
        sweep(add_rows, 0, c)
    for copy in sent:
        if any(copy is w for w in rows2[:HOLD2]):
            continue
        if any(copy is w for w in waits):
            pl.when(jnp.logical_not(late))(copy.wait_send)
        else:
            copy.wait_send()


def shards(
    adjoint_final,
    state_start,
    state_middle,
    speeds,
    flags,
    zones,
    growth_rate,
    transfer_rate,
    nucleation_rate,
):
    dims = adjoint_final.shape
    moms, sections = dims[0], dims[1]
    flat = (moms, sections, 8, 128)
    hbm = pl.BlockSpec(memory_space=pltpu.MemorySpace.HBM)
    vmem = pltpu.VMEM
    dma = pltpu.SemaphoreType.DMA
    out = pl.pallas_call(
        kernel,
        out_shape=jax.ShapeDtypeStruct(flat, F32),
        in_specs=[hbm] * 10,
        out_specs=pl.BlockSpec(memory_space=pltpu.VMEM),
        scratch_shapes=[
            vmem((moms, sections + 1, 8, 128), F32),
            vmem((moms, sections + 1, 8, 128), F32),
            vmem(flat, jnp.bfloat16),
            vmem(flat, jnp.bfloat16),
            vmem((3, 8, 128), F32),
            vmem((3, 8, 128), jnp.int32),
            vmem((8, 128), jnp.int32),
            pltpu.SMEM(growth_rate.shape, F32),
            pltpu.SMEM(transfer_rate.shape, F32),
            pltpu.SMEM(nucleation_rate.shape, F32),
            vmem((8, 128), F32),
            vmem((8, 128), F32),
            vmem((8, 128), F32),
            vmem((8, 128), F32),
            vmem((2, moms, sections, 4, 128), F32),
            vmem((moms, sections, 2, 4, 128), F32),
            vmem((moms, sections, 2, 4, 128), F32),
            vmem((sections, 8, 128), F32),
            vmem((sections, 8, 128), F32),
            vmem((sections, 8, 128), F32),
            vmem((sections, 8, 128), F32),
            vmem((5, 8, 128), F32),
            vmem((2, 5, 8, 128), F32),
            vmem((4, 8, 128), F32),
            vmem((2, 4, 8, 128), F32),
            dma((9,)),
            dma((REMOTE,)),
            dma((REMOTE,)),
        ],
        compiler_params=pltpu.CompilerParams(
            collective_id=0, has_side_effects=True, vmem_limit_bytes=40 << 20
        ),
    )(*[
        pltpu.with_memory_space_constraint(x, pltpu.MemorySpace.HBM)
        for x in (
            adjoint_final,
            adjoint_final.reshape(flat),
            state_middle.reshape(flat),
            state_start.reshape(flat),
            speeds.reshape(3, 8, 128),
            flags.reshape(3, 8, 128),
            zones.reshape(8, 128),
            growth_rate,
            transfer_rate,
            nucleation_rate,
        )
    ])
    return out.reshape(dims)


def solution(mesh):
    return jax.shard_map(
        shards,
        mesh=mesh,
        in_specs=(
            P(None, None, "azim", "axial", "rad"),
            P(None, None, "azim", "axial", "rad"),
            P(None, None, "azim", "axial", "rad"),
            P(None, "azim", "axial", "rad"),
            P(None, "azim", "axial", "rad"),
            P("azim", "axial", "rad"),
            P(),
            P(),
            P(),
        ),
        out_specs=P(None, None, "azim", "axial", "rad"),
        check_vma=False,
    )
```
